256 devices in a mesh: dp: 4 (over x), expert: 64 (over y, z, core).
Axes of the slice: x: 4, y: 4, z: 8, core: 2. Of those that a mesh axis runs over, the one named last changes fastest.
Arguments:
- tokens: bfloat16 [32768, 2048], P(('dp', 'expert')), may hold values from -6 to 6
- cotangent: bfloat16 [32768, 2048], P(('dp', 'expert')), may hold values from -6 to 6
- routes: int32 [32768, 8], P(('dp', 'expert')), may hold values from 0 to 63, all different within a row; in each aligned block of 128 rows (0 to 127, 128 to 255, ...) at most 18 rows name the same one
- probs: bfloat16 [32768, 8], P(('dp', 'expert')), may hold values from 0.019897461 to 0.29882812
- slot_expert: int32 [64], replicated, may hold values from 0 to 63, each once
- gate_w: bfloat16 [64, 2048, 384], P('expert', 'dp'), may hold values from -0.125 to 0.125
- up_w: bfloat16 [64, 2048, 384], P('expert', 'dp'), may hold values from -0.125 to 0.125
- down_w: bfloat16 [64, 384, 2048], P('expert', None, 'dp'), may hold values from -0.3125 to 0.3125
Outputs:
- grad_tokens: bfloat16 [32768, 2048], P(('dp', 'expert'))
- grad_probs: bfloat16 [32768, 8], P(('dp', 'expert'))
- grad_gate: float32 [64, 2048, 384], P('expert', 'dp')
- grad_up: float32 [64, 2048, 384], P('expert', 'dp')
- grad_down: float32 [64, 384, 2048], P('expert', None, 'dp')
The draws below stay inside these ranges and needn't reach their ends.
Inputs may be any that keep to these rules, and one draw needn't show every extreme that they name: `routes`: in each aligned block of 128 rows (the tokens of one device) no expert is named by more than 18 rows, a bound that some block reaches; a row names 8 different experts. `slot_expert`: each expert stands in exactly one slot.
All inputs are finite; a program needn't handle non-finite values.
Results may differ from the reference program's by a relative error of at most 0.008.
Values may be sent and summed in bfloat16 or wider, within the bound.
A program may use at most 128 MiB of HBM per device.

```python
import math
import jax
import jax.numpy as jnp
import numpy as np
from jax import lax

D = 2048
FF = 384
EXPERTS = 64
TOPK = 8
TOK_DEV = 128
CAP = 18
TOKENS = 32768


def block_scale(own_key, shape, split, low, high):
    def one(dim, blocks):
        draws = jax.random.uniform(jax.random.fold_in(jax.random.fold_in(own_key, 6), dim), (blocks,), jnp.float32, low / len(split), high / len(split))
        return jnp.repeat(jnp.exp(draws), shape[dim] // blocks).reshape((-1,) + (1,) * (len(shape) - dim - 1))

    factor_of = one(*split[0])
    for cut in split[1:]:
        factor_of = factor_of * one(*cut)
    return factor_of


def routed_block(key, own, number, rows, amount, top, limit, slope):
    sequence = jax.random.permutation(key, amount)
    packed, common = shares(amount, rows * top, limit, slope, True), shares(amount, rows * top, limit, slope, False)
    places = jnp.arange(amount)

    def named(sizes, rotation):
        used = int((sizes > 0).sum())
        fixed = max(1, used // 4)
        passed = fixed + (places - fixed + rotation * (used - fixed)) % max(1, amount - fixed)
        return jnp.zeros((amount,), jnp.int32).at[sequence[jnp.where(places < fixed, places, passed)]].set(jnp.asarray(sizes, jnp.int32))

    sizes = jnp.where(number % 4 == 0, named(packed, number // 4), named(common, number - number // 4 - 1))
    mixed = jax.random.permutation(jax.random.fold_in(own, 3), amount)
    donor, receiver = mixed[0:amount // 2 * 2:2], mixed[1:amount // 2 * 2:2]
    slack = jnp.minimum(sizes[donor] - 1, limit - sizes[receiver]) // 2
    slack = jnp.where((donor == sequence[0]) | (receiver == sequence[0]) | (sizes[receiver] == 0), 0, jnp.maximum(slack, 0))
    passed = jax.random.randint(jax.random.fold_in(own, 4), (amount // 2,), 0, 1 << 20) % (slack + 1)
    sizes = sizes.at[donor].add(-passed).at[receiver].add(passed)
    items = jnp.searchsorted(jnp.cumsum(sizes), jnp.arange(rows * top), side="right").astype(jnp.int32)
    grid = items.reshape(top, rows).T
    grid = grid[jax.random.permutation(jax.random.fold_in(own, 1), rows)]
    rotation = jax.random.randint(jax.random.fold_in(own, 2), (rows, 1), 0, top)
    return jnp.take_along_axis(grid, (jnp.arange(top)[None, :] + rotation) % top, axis=1)


def shares(amount, total, limit, skew, full):
    loads = [(1 << 20) // math.isqrt(rank ** skew) + 1 for rank in range(1, amount + 1)]
    largest = limit if full else min(limit, max(-(-total // amount), total * loads[0] // sum(loads)))
    least = 1 if total - largest >= amount - 1 else 0
    counts, surplus = [largest] + [least] * (amount - 1), total - largest - least * (amount - 1)
    while surplus > 0:
        movable = [i for i in range(1, amount) if counts[i] < largest] or [i for i in range(1, amount) if counts[i] < limit]
        pool, left = sum([loads[i] for i in movable]), surplus
        for i in movable:
            addition = min(limit - counts[i], max(1, left * loads[i] // pool), surplus)
            counts[i] = counts[i] + addition
            surplus = surplus - addition
    return np.array(counts)


def centred(key, extent, scale, reach, pieces=(), kind=jnp.bfloat16):
    array = scale * jax.random.normal(key, extent, jnp.float32)
    if pieces:
        array = array * block_scale(key, extent, pieces, -0.22, 0.18)
    return jnp.clip(array, -reach, reach).astype(kind)


def setup_inputs(seed: int = 0) -> dict:
    streams_of = jax.random.split(jax.random.key(seed), 9)
    tokens = centred(streams_of[0], (TOKENS, D), 1.0, 6.0, ((0, 256),))
    cotangent = centred(streams_of[1], (TOKENS, D), 1.0, 6.0, ((0, 256),))
    routes_keys = jax.random.split(jax.random.fold_in(streams_of[2], 1), TOKENS // TOK_DEV)
    routes_turns = jax.random.permutation(jax.random.fold_in(streams_of[2], 3), TOKENS // TOK_DEV)
    routes = jax.vmap(lambda own, number: routed_block(jax.random.fold_in(streams_of[2], 2), own, number, TOK_DEV, EXPERTS, TOPK, CAP, 2))(routes_keys, routes_turns).reshape((TOKENS, TOPK))
    probs = jnp.clip(0.019897461 + 0.27893066 * jax.random.uniform(streams_of[3], (TOKENS, TOPK), jnp.float32) ** block_scale(streams_of[3], (TOKENS, TOPK), ((0, 256),), -0.2, 0.2), 0.019897461, 0.29882812).astype(jnp.bfloat16)
    slot_expert = jax.random.permutation(streams_of[4], EXPERTS).astype(jnp.int32)
    gate_w = centred(streams_of[5], (EXPERTS, D, FF), D ** -0.5, 0.125, ((0, 64), (1, 4)))
    up_w = centred(streams_of[6], (EXPERTS, D, FF), D ** -0.5, 0.125, ((0, 64), (1, 4)))
    down_w = centred(streams_of[7], (EXPERTS, FF, D), FF ** -0.5, 0.3125, ((0, 64), (2, 4)))
    return dict(tokens=tokens, cotangent=cotangent, routes=routes, probs=probs, slot_expert=slot_expert, gate_w=gate_w, up_w=up_w, down_w=down_w)


def reference(tokens, cotangent, routes, probs, slot_expert, gate_w, up_w, down_w):
    n_src = TOKENS // TOK_DEV
    total = TOKENS * TOPK
    flat = routes.reshape(n_src, TOK_DEV * TOPK).astype(jnp.int32)
    labels = jnp.arange(EXPERTS, dtype=jnp.int32)
    onehot = (flat[:, :, None] == labels[None, None, :]).astype(jnp.int32)
    before = jnp.cumsum(onehot, axis=1) - onehot
    position = jnp.sum(before * onehot, axis=2).astype(jnp.int32)
    assign = jnp.arange(total, dtype=jnp.int32).reshape(n_src, TOK_DEV * TOPK)
    source = jnp.broadcast_to(jnp.arange(n_src, dtype=jnp.int32)[:, None], flat.shape)
    table = jnp.full((EXPERTS, n_src, CAP), total, jnp.int32)
    table = table.at[flat, source, position].set(assign).reshape(EXPERTS, n_src * CAP)
    x_pad = jnp.concatenate([tokens, jnp.zeros((1, D), jnp.bfloat16)], axis=0)
    dy_pad = jnp.concatenate([cotangent, jnp.zeros((1, D), jnp.bfloat16)], axis=0)
    p_pad = jnp.concatenate([probs.reshape(-1), jnp.zeros((1,), jnp.bfloat16)], axis=0)

    def one_slot(carry, slot):
        dx_acc, dp_acc = carry
        expert_id = slot_expert[slot]
        index = table[expert_id]
        token_row = jnp.minimum(index // TOPK, TOKENS).astype(jnp.int32)
        x_rows = x_pad[token_row]
        dy_rows = dy_pad[token_row]
        weight = p_pad[index].astype(jnp.float32)[:, None]
        w_gate = gate_w[slot]
        w_up = up_w[slot]
        w_down = down_w[slot]
        gate = jnp.dot(x_rows, w_gate, preferred_element_type=jnp.float32)
        upval = jnp.dot(x_rows, w_up, preferred_element_type=jnp.float32)
        sig = jax.nn.sigmoid(gate)
        act = gate * sig
        hidden = (act * upval).astype(jnp.bfloat16)
        back = jnp.dot(dy_rows, w_down.T, preferred_element_type=jnp.float32)
        dprob = jnp.sum(hidden.astype(jnp.float32) * back, axis=1).astype(jnp.bfloat16)
        dh = weight * back
        d_gate = (dh * upval * sig * (1.0 + gate * (1.0 - sig))).astype(jnp.bfloat16)
        d_up = (dh * act).astype(jnp.bfloat16)
        dx_rows = (jnp.dot(d_gate, w_gate.T, preferred_element_type=jnp.float32)
                   + jnp.dot(d_up, w_up.T, preferred_element_type=jnp.float32)).astype(jnp.bfloat16)
        wdy = (weight * dy_rows.astype(jnp.float32)).astype(jnp.bfloat16)
        g_gate = jnp.dot(x_rows.T, d_gate, preferred_element_type=jnp.float32)
        g_up = jnp.dot(x_rows.T, d_up, preferred_element_type=jnp.float32)
        g_down = jnp.dot(hidden.T, wdy, preferred_element_type=jnp.float32)
        dx_acc = dx_acc.at[token_row].add(dx_rows.astype(jnp.float32))
        dp_acc = dp_acc.at[index].add(dprob.astype(jnp.float32))
        return (dx_acc, dp_acc), (g_gate, g_up, g_down)

    start = (jnp.zeros((TOKENS + 1, D), jnp.float32), jnp.zeros((total + 1,), jnp.float32))
    (dx_acc, dp_acc), (grad_gate, grad_up, grad_down) = lax.scan(one_slot, start, jnp.arange(EXPERTS, dtype=jnp.int32))
    grad_tokens = dx_acc[:TOKENS].astype(jnp.bfloat16)
    grad_probs = dp_acc[:total].reshape(TOKENS, TOPK).astype(jnp.bfloat16)
    return (grad_tokens, grad_probs, grad_gate, grad_up, grad_down)
```

```python
import functools

import jax
import jax.numpy as jnp
from jax import lax
from jax.experimental import pallas as pl
from jax.experimental.pallas import tpu as pltpu
from jax.sharding import PartitionSpec as P

CAP = 18
NX, NY, NZ, NC = 4, 4, 8, 2
PLANE = NY * NC
ROWS = NZ * CAP
MESH = pl.DeviceIdType.MESH
F32 = jnp.float32
BF16 = jnp.bfloat16


def mod(a, n):
    return lax.rem(a + n, n)


class Place:
    def __init__(self):
        self.x = lax.axis_index("dp")
        e = lax.axis_index("expert")
        self.c = lax.rem(e, NC)
        self.z = lax.rem(lax.div(e, NC), NZ)
        self.y = lax.div(e, NC * NZ)
        self.plane = self.y * NC + self.c

    def dev(self, y, z, c):
        return {"expert": (y * NZ + z) * NC + c}

    def at_z(self, step):
        return self.dev(self.y, mod(self.z + step, NZ), self.c)

    def at_y(self, step, c):
        return self.dev(mod(self.y + step, NY), self.z, c)

    def at_x(self, step):
        return {"dp": mod(self.x + step, NX)}

    def peers(self):
        out = [self.at_z(s) for s in range(1, NZ)]
        out += [self.at_y(s, c) for s in (1, -1) for c in range(NC)]
        out += [self.at_y(0, 1 - self.c), self.at_x(1), self.at_x(-1)]
        return out


def greet(me):
    barrier = pltpu.get_barrier_semaphore()
    peers = me.peers()
    for peer in peers:
        pl.semaphore_signal(barrier, inc=1, device_id=peer, device_id_type=MESH)
    pl.semaphore_wait(barrier, len(peers))


def remote(src, dst, send, recv, dev):
    return pltpu.make_async_remote_copy(
        src_ref=src, dst_ref=dst, send_sem=send, recv_sem=recv, device_id=dev, device_id_type=MESH
    )


def plane_send(me, piece, landing, relay, send, recv, relay_recv):
    for step, core in ((1, 0), (-1, 1)):
        remote(
            piece(mod(me.y + 2, NY) * NC + core), relay(core), send, relay_recv(core), me.at_y(step, me.c)
        ).start()
    for step in (1, -1):
        for core in range(NC):
            there = mod(me.y + step, NY)
            remote(piece(there * NC + core), landing(me.plane), send, recv, me.at_y(step, core)).start()
    remote(piece(me.y * NC + 1 - me.c), landing(me.plane), send, recv, me.at_y(0, 1 - me.c)).start()


def plane_relay(me, landing, relay, send, recv, relay_recv):
    for step, core in ((1, 0), (-1, 1)):
        remote(relay(core), relay(core), send, relay_recv(core), me.at_y(step, core)).wait_recv()
        origin = mod(me.y - step, NY) * NC + me.c
        remote(relay(core), landing(origin), send, recv, me.at_y(step, core)).start()


def dispatch_kernel(
    width,
    chunks,
    tok,
    cot,
    routes,
    probs,
    slots,
    gate,
    up,
    down,
    out_x,
    out_dy,
    out_p,
    all_gate,
    all_up,
    all_down,
    key_out,
    zbuf,
    sbuf,
    relay,
    maps_own,
    maps,
    pick,
    pbuf,
    prelay,
    own_sem,
    map_send,
    map_recv,
    z_send,
    z_recv,
    y_send,
    y_recv,
    r_recv,
    y_own,
    w_send,
    w_recv,
    w_own,
):
    me = Place()
    cw = width // chunks
    half = cw // 2
    total = 2 * chunks
    rows = tok.shape[0]

    def own_copy(k):
        src = (tok, cot)[k // chunks]
        return pltpu.make_async_copy(
            src.at[:, pl.ds((k % chunks) * cw, cw)], zbuf.at[k, me.z], own_sem.at[k]
        )

    for k in range(total):
        own_copy(k).start()

    hit = jnp.zeros((NZ * PLANE, rows), F32)
    weight = jnp.zeros((NZ * PLANE, rows), F32)
    named = slots[...]
    for k in range(routes.shape[0]):
        same = named == routes[k : k + 1, :]
        hit = hit + jnp.where(same, 1.0, 0.0)
        weight = weight + jnp.where(same, probs[k : k + 1, :], 0.0)
    before = lax.broadcasted_iota(jnp.int32, (rows, rows), 0) < lax.broadcasted_iota(
        jnp.int32, (rows, rows), 1
    )
    rank = jnp.dot(
        hit.astype(BF16), jnp.where(before, 1.0, 0.0).astype(BF16), preferred_element_type=F32
    )
    row_of = jnp.where(hit > 0.5, rank + (me.z * CAP).astype(F32), -1.0)
    for z in range(NZ):
        maps_own[z, 0] = row_of[z * PLANE : (z + 1) * PLANE]
        maps_own[z, 1] = weight[z * PLANE : (z + 1) * PLANE]
    maps[me.z] = maps_own[me.z]
    for k in range(total):
        own_copy(k).wait()

    greet(me)

    def z_copy(k, direction, stage):
        sign = 1 - 2 * direction
        block = mod(me.z - sign * stage, NZ)
        if stage == 3:
            where = zbuf.at[k, block, :, pl.ds(direction * half, half)]
        else:
            where = zbuf.at[k, block]
        return remote(
            where, where, z_send.at[k, direction, stage], z_recv.at[k, direction, stage], me.at_z(sign)
        )

    def z_wait(k, direction, stage):
        sign = 1 - 2 * direction
        block = mod(me.z - sign * (stage + 1), NZ)
        if stage == 3:
            where = zbuf.at[k, block, :, pl.ds(direction * half, half)]
        else:
            where = zbuf.at[k, block]
        remote(
            where, where, z_send.at[k, direction, stage], z_recv.at[k, direction, stage], me.at_z(sign)
        ).wait_recv()

    def z_stage(k, stage):
        for direction in (0, 1):
            if stage > 0:
                z_wait(k, direction, stage - 1)
            if stage < 4:
                z_copy(k, direction, stage).start()

    weights = ((gate, all_gate, True), (up, all_up, True), (down, all_down, False))

    def w_slot(n, owner):
        src, dst, lead = weights[n]
        if lead:
            return dst.at[owner]
        return dst.at[:, pl.ds(pl.multiple_of(owner * src.shape[1], 128), src.shape[1])]

    def w_copy(n, direction, hop):
        sign = 1 - 2 * direction
        owner = me.x if hop == 0 else mod(me.x - sign, NX)
        src = weights[n][0] if hop == 0 else w_slot(n, owner)
        return remote(
            src, w_slot(n, owner), w_send.at[n, direction, hop], w_recv.at[n, direction, hop], me.at_x(sign)
        )

    def w_wait(n, direction, hop):
        sign = 1 - 2 * direction
        slot = w_slot(n, mod(me.x - sign * (hop + 1), NX))
        remote(
            slot, slot, w_send.at[n, direction, hop], w_recv.at[n, direction, hop], me.at_x(sign)
        ).wait_recv()

    for s in range(1, NZ):
        z = mod(me.z + s, NZ)
        remote(maps_own.at[z], maps.at[me.z], map_send.at[s], map_recv.at[s], me.at_z(s)).start()
    z_stage(0, 0)
    for n in range(3):
        for direction in (0, 1):
            w_copy(n, direction, 0).start()
        pltpu.make_async_copy(weights[n][0], w_slot(n, me.x), w_own.at[n]).start()

    for s in range(1, NZ):
        z = mod(me.z - s, NZ)
        remote(maps.at[z], maps.at[z], map_send.at[s], map_recv.at[s], me.at_z(s)).wait_recv()
    row = lax.broadcasted_iota(jnp.int32, (ROWS, rows), 0).astype(F32)
    ones = jnp.ones((rows, rows), BF16)
    for d in range(PLANE):
        share = jnp.zeros((ROWS, rows), F32)
        for z in range(NZ):
            taken = maps[z, 0, d : d + 1, :] == row
            pick[d * ROWS : (d + 1) * ROWS, z * rows : (z + 1) * rows] = jnp.where(taken, 1.0, 0.0).astype(BF16)
            share = share + jnp.where(taken, maps[z, 1, d : d + 1, :], 0.0)
            key_out[d : d + 1, z * rows : (z + 1) * rows] = maps[z, 0, d : d + 1, :]
        pbuf[d] = jnp.dot(share.astype(BF16), ones, preferred_element_type=F32).astype(BF16)

    last = total

    def piece(k):
        return lambda d: sbuf.at[k, d]

    def relay_of(k):
        return lambda core: relay.at[k, core]

    def relay_sem(k):
        return lambda core: r_recv.at[k, core]

    def landing(k, out):
        col = pl.multiple_of(lax.rem(k, chunks) * cw, cw)
        return lambda slot: out.at[slot, :, pl.ds(col, cw)]

    def by_array(k, act):
        @pl.when(k < chunks)
        def _():
            act(out_x)

        @pl.when(k >= chunks)
        def _():
            act(out_dy)

    def send_chunk(k):
        def act(out):
            plane_send(
                me, piece(k), landing(k, out), relay_of(k), y_send.at[k], y_recv.at[k], relay_sem(k)
            )
            pltpu.make_async_copy(
                sbuf.at[k, me.plane], landing(k, out)(me.plane), y_own.at[k]
            ).start()

        by_array(k, act)

    def relay_chunk(k):
        by_array(
            k,
            lambda out: plane_relay(
                me, landing(k, out), relay_of(k), y_send.at[k], y_recv.at[k], relay_sem(k)
            ),
        )

    def p_land(slot):
        return out_p.at[slot]

    def p_relay(core):
        return prelay.at[core]

    def p_sem(core):
        return r_recv.at[last, core]

    def step(i, carry):
        @pl.when((i >= 1) & (i < total))
        def _():
            z_stage(i, 0)

        @pl.when((i >= 1) & (i <= total))
        def _():
            z_stage(i - 1, 2)

        @pl.when((i >= 2) & (i <= total + 1))
        def _():
            k = i - 2
            z_stage(k, 4)
            block = zbuf[k].reshape(NZ * rows, cw)
            out = jnp.dot(pick[...], block, preferred_element_type=F32).astype(BF16)
            sbuf[k] = out.reshape(PLANE, ROWS, cw)
            send_chunk(k)

        @pl.when(i < total)
        def _():
            z_stage(i, 1)

        @pl.when((i >= 1) & (i <= total))
        def _():
            z_stage(i - 1, 3)

        @pl.when((i >= 3) & (i <= total + 2))
        def _():
            relay_chunk(i - 3)

        @pl.when(i == 1)
        def _():
            for n in range(3):
                for direction in (0, 1):
                    w_wait(n, direction, 0)
                w_copy(n, 0 if n < 2 else 1, 1).start()

        @pl.when(i == 2)
        def _():
            plane_send(me, lambda d: pbuf.at[d], p_land, p_relay, y_send.at[last], y_recv.at[last], p_sem)
            pltpu.make_async_copy(pbuf.at[me.plane], out_p.at[me.plane], y_own.at[last]).start()

        @pl.when(i == 3)
        def _():
            plane_relay(me, p_land, p_relay, y_send.at[last], y_recv.at[last], p_sem)

        return carry

    lax.fori_loop(0, total + 3, step, 0)

    for n in range(3):
        w_wait(n, 0 if n < 2 else 1, 1)
        for direction in (0, 1):
            w_copy(n, direction, 0).wait_send()
        w_copy(n, 0 if n < 2 else 1, 1).wait_send()
        pltpu.make_async_copy(weights[n][0], w_slot(n, me.x), w_own.at[n]).wait()
    for s in range(1, NZ):
        z = mod(me.z + s, NZ)
        remote(maps_own.at[z], maps.at[me.z], map_send.at[s], map_recv.at[s], me.at_z(s)).wait_send()

    def drain(k, carry):
        for direction in (0, 1):
            for stage in range(4):
                z_copy(k, direction, stage).wait_send()

        def act(out):
            here = out.at[pl.ds(0, PLANE - 1), :, pl.ds(pl.multiple_of(lax.rem(k, chunks) * cw, cw), cw)]
            sent = sbuf.at[k, pl.ds(0, PLANE - 1)]
            remote(sent, here, y_send.at[k], y_recv.at[k], me.at_y(1, 0)).wait_recv()
            remote(sent, here, y_send.at[k], y_recv.at[k], me.at_y(1, 0)).wait_send()
            two = sbuf.at[k, pl.ds(0, 2)]
            remote(two, two, y_send.at[k], y_recv.at[k], me.at_y(1, 0)).wait_send()
            pltpu.make_async_copy(
                sbuf.at[k, me.plane], landing(k, out)(me.plane), y_own.at[k]
            ).wait()

        by_array(k, act)
        return carry

    lax.fori_loop(0, total, drain, 0)
    here, sent, two = out_p.at[pl.ds(0, PLANE - 1)], pbuf.at[pl.ds(0, PLANE - 1)], pbuf.at[pl.ds(0, 2)]
    remote(sent, here, y_send.at[last], y_recv.at[last], me.at_y(1, 0)).wait_recv()
    remote(sent, here, y_send.at[last], y_recv.at[last], me.at_y(1, 0)).wait_send()
    remote(two, two, y_send.at[last], y_recv.at[last], me.at_y(1, 0)).wait_send()
    pltpu.make_async_copy(pbuf.at[me.plane], out_p.at[me.plane], y_own.at[last]).wait()


def dispatch(tokens, cotangent, routes, probs, slots, gate, up, down, chunks=4):
    rows, width = tokens.shape
    depth, ff = gate.shape
    cw, total = width // chunks, 2 * chunks
    dma = pltpu.SemaphoreType.DMA
    vmem = pl.BlockSpec(memory_space=pltpu.VMEM)
    anyp = pl.BlockSpec(memory_space=pl.ANY)
    shape = jax.ShapeDtypeStruct
    return pl.pallas_call(
        functools.partial(dispatch_kernel, width, chunks),
        out_shape=(
            shape((PLANE, ROWS, width), BF16),
            shape((PLANE, ROWS, width), BF16),
            shape((PLANE, ROWS, rows), BF16),
            shape((NX, depth, ff), BF16),
            shape((NX, depth, ff), BF16),
            shape((ff, width), BF16),
            shape((PLANE, NZ * rows), F32),
        ),
        in_specs=[anyp, anyp, vmem, vmem, vmem, vmem, vmem, vmem],
        out_specs=(anyp, anyp, anyp, anyp, anyp, anyp, vmem),
        scratch_shapes=[
            pltpu.VMEM((total, NZ, rows, cw), BF16),
            pltpu.VMEM((total, PLANE, ROWS, cw), BF16),
            pltpu.VMEM((total, 2, ROWS, cw), BF16),
            pltpu.VMEM((NZ, 2, PLANE, rows), F32),
            pltpu.VMEM((NZ, 2, PLANE, rows), F32),
            pltpu.VMEM((PLANE * ROWS, NZ * rows), BF16),
            pltpu.VMEM((PLANE, ROWS, rows), BF16),
            pltpu.VMEM((2, ROWS, rows), BF16),
            dma((total,)),
            dma((NZ,)),
            dma((NZ,)),
            dma((total, 2, 4)),
            dma((total, 2, 4)),
            dma((total + 1,)),
            dma((total + 1,)),
            dma((total + 1, 2)),
            dma((total + 1,)),
            dma((3, 2, 2)),
            dma((3, 2, 2)),
            dma((3,)),
        ],
        compiler_params=pltpu.CompilerParams(
            collective_id=0, has_side_effects=True, vmem_limit_bytes=60 * 1024 * 1024
        ),
        name="dispatch",
    )(tokens, cotangent, routes, probs, slots, gate, up, down)


def combine_kernel(
    width,
    chunks,
    dx,
    dp,
    key,
    routes,
    slots,
    part_gate,
    part_up,
    part_down,
    out_tok,
    out_prob,
    out_gate,
    out_up,
    out_down,
    rbuf,
    relay,
    spread,
    gbuf,
    zout,
    zin,
    pbuf,
    prelay,
    maps_own,
    maps,
    wbuf0,
    wbuf1,
    wbuf2,
    wout0,
    wout1,
    wout2,
    win0,
    win1,
    win2,
    map_send,
    map_recv,
    z_send,
    z_recv,
    y_send,
    y_recv,
    r_recv,
    y_own,
    w_send,
    w_recv,
    w_own,
):
    me = Place()
    cw = width // chunks
    half = cw // 2
    rows = out_tok.shape[0]
    last = chunks
    parts = ((part_gate, wbuf0, wout0, win0, out_gate), (part_up, wbuf1, wout1, win1, out_up))
    parts = parts + ((part_down, wbuf2, wout2, win2, out_down),)
    way = (1, -1, 1)

    def w_block(n, owner):
        src = parts[n][0]
        if n < 2:
            return src.at[pl.ds(pl.multiple_of(owner * out_gate.shape[0], 128), out_gate.shape[0])]
        return src.at[:, pl.ds(pl.multiple_of(owner * out_down.shape[1], 128), out_down.shape[1])]

    def w_load(n, b):
        return pltpu.make_async_copy(w_block(n, mod(me.x + b, NX)), parts[n][1].at[b], w_own.at[n, b])

    for n in range(3):
        for b in range(NX):
            w_load(n, b).start()

    lane = lax.broadcasted_iota(jnp.int32, (NZ * rows, 128), 1).astype(F32)
    turned = key[...].T
    for j in range(PLANE * ROWS // 128):
        tile = jnp.zeros((NZ * rows, 128), F32)
        for d in range(128 * j // ROWS, (128 * j + 127) // ROWS + 1):
            mine = turned[:, d : d + 1]
            where = jnp.where(mine >= 0.0, mine + float(d * ROWS - 128 * j), -1.0)
            tile = tile + jnp.where(where == lane, 1.0, 0.0)
        spread[:, j * 128 : (j + 1) * 128] = tile.astype(BF16)

    greet(me)

    def cols(k):
        return pl.ds(pl.multiple_of(k * cw, cw), cw)

    def piece(k):
        return lambda d: dx.at[d, :, cols(k)]

    def landing(k):
        return lambda slot: rbuf.at[k, slot]

    def relay_of(k):
        return lambda core: relay.at[k, core]

    def relay_sem(k):
        return lambda core: r_recv.at[k, core]

    def y_start(k):
        plane_send(me, piece(k), landing(k), relay_of(k), y_send.at[k], y_recv.at[k], relay_sem(k))
        pltpu.make_async_copy(piece(k)(me.plane), rbuf.at[k, me.plane], y_own.at[k]).start()

    def y_pass(k):
        plane_relay(me, landing(k), relay_of(k), y_send.at[k], y_recv.at[k], relay_sem(k))

    def p_land(slot):
        return pbuf.at[slot]

    def p_relay(core):
        return prelay.at[core]

    def p_sem(core):
        return r_recv.at[last, core]

    plane_send(me, lambda d: dp.at[d], p_land, p_relay, y_send.at[last], y_recv.at[last], p_sem)
    pltpu.make_async_copy(dp.at[me.plane], pbuf.at[me.plane], y_own.at[last]).start()
    y_start(0)
    plane_relay(me, p_land, p_relay, y_send.at[last], y_recv.at[last], p_sem)

    def w_copy(n, hop):
        sign = way[n] if hop < 2 else -way[n]
        return remote(
            parts[n][2].at[hop], parts[n][3].at[hop], w_send.at[n, hop], w_recv.at[n, hop], me.at_x(sign)
        )

    def w_first():
        for n in range(3):
            for b in range(NX):
                w_load(n, b).wait()
            parts[n][2][0] = parts[n][1][2].astype(BF16)
            parts[n][2][2] = parts[n][1][(NX - way[n]) % NX].astype(BF16)
        for n in range(3):
            w_copy(n, 0).start()
            w_copy(n, 2).start()

    def w_second():
        for n in range(3):
            w_copy(n, 0).wait_recv()
            summed = parts[n][1][way[n] % NX] + parts[n][3][0].astype(F32)
            parts[n][2][1] = summed.astype(BF16)
        for n in range(3):
            w_copy(n, 1).start()

    def w_third():
        for n in range(3):
            w_copy(n, 1).wait_recv()
            w_copy(n, 2).wait_recv()
            parts[n][4][...] = parts[n][1][0] + parts[n][3][1].astype(F32) + parts[n][3][2].astype(F32)

    w_first()

    def z_copy(k, direction, stage):
        sign = 1 - 2 * direction
        if stage == 0:
            part = pl.ds(direction * half, half)
            src, dst = zout.at[k, direction, 0, :, part], zin.at[k, direction, 0, :, part]
        else:
            src, dst = zout.at[k, direction, stage], zin.at[k, direction, stage]
        return remote(src, dst, z_send.at[k, direction, stage], z_recv.at[k, direction, stage], me.at_z(sign))

    def z_stage(k, stage):
        for direction in (0, 1):
            sign = 1 - 2 * direction
            block = mod(me.z + sign * (4 - stage), NZ)
            if stage == 0:
                part = slice(direction * half, (direction + 1) * half)
                zout[k, direction, 0, :, part] = gbuf[k, block, :, part].astype(BF16)
            else:
                z_copy(k, direction, stage - 1).wait_recv()
                if stage == 1:
                    near = slice(direction * half, (direction + 1) * half)
                    rest = slice((1 - direction) * half, (2 - direction) * half)
                    summed = gbuf[k, block, :, near] + zin[k, direction, 0, :, near].astype(F32)
                    zout[k, direction, 1, :, near] = summed.astype(BF16)
                    zout[k, direction, 1, :, rest] = gbuf[k, block, :, rest].astype(BF16)
                else:
                    summed = gbuf[k, block] + zin[k, direction, stage - 1].astype(F32)
                    zout[k, direction, stage] = summed.astype(BF16)
            z_copy(k, direction, stage).start()

    def z_finish(k):
        z_copy(k, 0, 3).wait_recv()
        z_copy(k, 1, 3).wait_recv()
        summed = gbuf[k, me.z] + zin[k, 0, 3].astype(F32) + zin[k, 1, 3].astype(F32)
        out_tok[:, cols(k)] = summed.astype(BF16)

    def y_wait(k):
        seven = rbuf.at[k, pl.ds(0, PLANE - 1)]
        remote(seven, seven, y_send.at[k], y_recv.at[k], me.at_y(1, 0)).wait_recv()
        pltpu.make_async_copy(piece(k)(me.plane), rbuf.at[k, me.plane], y_own.at[k]).wait()

    def map_copy(s):
        z = mod(me.z + s, NZ)
        return remote(maps_own.at[z], maps.at[me.z], map_send.at[s], map_recv.at[s], me.at_z(s))

    def prob_grads():
        seven = pbuf.at[pl.ds(0, PLANE - 1)]
        remote(seven, seven, y_send.at[last], y_recv.at[last], me.at_y(1, 0)).wait_recv()
        pltpu.make_async_copy(dp.at[me.plane], pbuf.at[me.plane], y_own.at[last]).wait()
        row = lax.broadcasted_iota(jnp.int32, (ROWS, rows), 0).astype(F32)
        for d in range(PLANE):
            given = pbuf[d].astype(F32)
            for z in range(NZ):
                taken = key[d : d + 1, z * rows : (z + 1) * rows] == row
                maps_own[z, d : d + 1, :] = jnp.sum(jnp.where(taken, given, 0.0), axis=0, keepdims=True)
        maps[me.z] = maps_own[me.z]
        for s in range(1, NZ):
            map_copy(s).start()

    def step(i, carry):
        @pl.when((i >= 1) & (i < chunks))
        def _():
            y_start(i)

        @pl.when((i >= 1) & (i <= chunks))
        def _():
            y_pass(i - 1)

        @pl.when((i >= 3) & (i <= chunks + 2))
        def _():
            z_stage(i - 3, 2)

        @pl.when((i >= 2) & (i <= chunks + 1))
        def _():
            k = i - 2
            y_wait(k)
            got = rbuf[k].reshape(PLANE * ROWS, cw)
            gbuf[k] = jnp.dot(spread[...], got, preferred_element_type=F32).reshape(NZ, rows, cw)
            z_stage(k, 0)

        @pl.when((i >= 3) & (i <= chunks + 2))
        def _():
            z_stage(i - 3, 3)

        @pl.when(i == 2)
        def _():
            prob_grads()

        @pl.when((i >= 2) & (i <= chunks + 1))
        def _():
            z_stage(i - 2, 1)

        @pl.when((i >= 3) & (i <= chunks + 2))
        def _():
            z_finish(i - 3)

        @pl.when(i == 3)
        def _():
            w_second()

        return carry

    lax.fori_loop(0, chunks + 3, step, 0)
    w_third()
    for s in range(1, NZ):
        z = mod(me.z - s, NZ)
        remote(maps.at[z], maps.at[z], map_send.at[s], map_recv.at[s], me.at_z(s)).wait_recv()
    named = slots[...]
    given = maps[...].reshape(NZ * PLANE, rows)
    for k in range(routes.shape[0]):
        same = named == routes[k : k + 1, :]
        out_prob[k : k + 1, :] = jnp.sum(jnp.where(same, given, 0.0), axis=0, keepdims=True)

    def drain(k, carry):
        for direction in (0, 1):
            for stage in range(4):
                z_copy(k, direction, stage).wait_send()
        seven, two = rbuf.at[k, pl.ds(0, PLANE - 1)], rbuf.at[k, pl.ds(0, 2)]
        remote(seven, seven, y_send.at[k], y_recv.at[k], me.at_y(1, 0)).wait_send()
        remote(two, two, y_send.at[k], y_recv.at[k], me.at_y(1, 0)).wait_send()
        return carry

    lax.fori_loop(0, chunks, drain, 0)
    seven, two = pbuf.at[pl.ds(0, PLANE - 1)], pbuf.at[pl.ds(0, 2)]
    remote(seven, seven, y_send.at[last], y_recv.at[last], me.at_y(1, 0)).wait_send()
    remote(two, two, y_send.at[last], y_recv.at[last], me.at_y(1, 0)).wait_send()
    for s in range(1, NZ):
        map_copy(s).wait_send()
    for n in range(3):
        for hop in range(3):
            w_copy(n, hop).wait_send()


def combine(dx, dp, key, routes, slots, part_gate, part_up, part_down, chunks=4):
    _, _, width = dx.shape
    rows = dp.shape[2]
    cw = width // chunks
    depth, ff = part_gate.shape[0] // NX, part_gate.shape[1]
    dma = pltpu.SemaphoreType.DMA
    vmem = pl.BlockSpec(memory_space=pltpu.VMEM)
    anyp = pl.BlockSpec(memory_space=pl.ANY)
    shape = jax.ShapeDtypeStruct
    one, two = (depth, ff), (ff, width // NX)
    return pl.pallas_call(
        functools.partial(combine_kernel, width, chunks),
        out_shape=(
            shape((rows, width), BF16),
            shape(routes.shape, F32),
            shape(one, F32),
            shape(one, F32),
            shape(two, F32),
        ),
        in_specs=[anyp, anyp, vmem, vmem, vmem, anyp, anyp, anyp],
        out_specs=(vmem, vmem, vmem, vmem, vmem),
        scratch_shapes=[
            pltpu.VMEM((chunks, PLANE, ROWS, cw), BF16),
            pltpu.VMEM((chunks, 2, ROWS, cw), BF16),
            pltpu.VMEM((NZ * rows, PLANE * ROWS), BF16),
            pltpu.VMEM((chunks, NZ, rows, cw), F32),
            pltpu.VMEM((chunks, 2, 4, rows, cw), BF16),
            pltpu.VMEM((chunks, 2, 4, rows, cw), BF16),
            pltpu.VMEM((PLANE, ROWS, rows), BF16),
            pltpu.VMEM((2, ROWS, rows), BF16),
            pltpu.VMEM((NZ, PLANE, rows), F32),
            pltpu.VMEM((NZ, PLANE, rows), F32),
            pltpu.VMEM((NX,) + one, F32),
            pltpu.VMEM((NX,) + one, F32),
            pltpu.VMEM((NX,) + two, F32),
            pltpu.VMEM((3,) + one, BF16),
            pltpu.VMEM((3,) + one, BF16),
            pltpu.VMEM((3,) + two, BF16),
            pltpu.VMEM((3,) + one, BF16),
            pltpu.VMEM((3,) + one, BF16),
            pltpu.VMEM((3,) + two, BF16),
            dma((NZ,)),
            dma((NZ,)),
            dma((chunks, 2, 4)),
            dma((chunks, 2, 4)),
            dma((chunks + 1,)),
            dma((chunks + 1,)),
            dma((chunks + 1, 2)),
            dma((chunks + 1,)),
            dma((3, 3)),
            dma((3, 3)),
            dma((3, NX)),
        ],
        compiler_params=pltpu.CompilerParams(
            collective_id=1, has_side_effects=True, vmem_limit_bytes=62 * 1024 * 1024
        ),
        name="combine",
    )(dx, dp, key, routes, slots, part_gate, part_up, part_down)


def shards(tokens, cotangent, routes, probs, slot_expert, gate_w, up_w, down_w):
    rows, width = tokens.shape
    ff = gate_w.shape[2]
    by_plane = slot_expert.reshape(NY, NZ, NC).transpose(1, 0, 2).reshape(-1)
    slots = jnp.broadcast_to(by_plane[:, None], (by_plane.shape[0], rows))
    turned = routes.T
    x, dy, p, w_gate, w_up, w_down, key = dispatch(
        tokens, cotangent, turned, probs.T.astype(F32), slots, gate_w[0], up_w[0], down_w[0]
    )
    total = PLANE * ROWS
    x, dy = x.reshape(total, width), dy.reshape(total, width)
    weight = p.reshape(total, rows)[:, :1].astype(F32)
    w_gate, w_up = w_gate.reshape(width, ff), w_up.reshape(width, ff)
    gate = jnp.dot(x, w_gate, preferred_element_type=F32)
    upval = jnp.dot(x, w_up, preferred_element_type=F32)
    sig = jax.nn.sigmoid(gate)
    act = gate * sig
    hidden = (act * upval).astype(BF16)
    back = lax.dot_general(dy, w_down, (((1,), (1,)), ((), ())), preferred_element_type=F32)
    dprob = jnp.sum(hidden.astype(F32) * back, axis=1, keepdims=True).astype(BF16)
    dh = weight * back
    d_gate = (dh * upval * sig * (1.0 + gate * (1.0 - sig))).astype(BF16)
    d_up = (dh * act).astype(BF16)
    wide = (((1,), (1,)), ((), ()))
    dx = (
        lax.dot_general(d_gate, w_gate, wide, preferred_element_type=F32)
        + lax.dot_general(d_up, w_up, wide, preferred_element_type=F32)
    ).astype(BF16)
    wdy = (weight * dy.astype(F32)).astype(BF16)
    tall = (((0,), (0,)), ((), ()))
    part_gate = lax.dot_general(x, d_gate, tall, preferred_element_type=F32)
    part_up = lax.dot_general(x, d_up, tall, preferred_element_type=F32)
    part_down = lax.dot_general(hidden, wdy, tall, preferred_element_type=F32)
    grad_tokens, grad_probs, grad_gate, grad_up, grad_down = combine(
        dx.reshape(PLANE, ROWS, width),
        jnp.broadcast_to(dprob, (total, rows)).reshape(PLANE, ROWS, rows),
        key,
        turned,
        slots,
        part_gate,
        part_up,
        part_down,
    )
    return (
        grad_tokens,
        grad_probs.T.astype(BF16),
        grad_gate[None],
        grad_up[None],
        grad_down[None],
    )


def solution(mesh):
    placed = (
        P(("dp", "expert"), None),
        P(("dp", "expert"), None),
        P(("dp", "expert"), None),
        P(("dp", "expert"), None),
        P(),
        P("expert", "dp", None),
        P("expert", "dp", None),
        P("expert", None, "dp"),
    )
    return jax.shard_map(
        shards,
        mesh=mesh,
        in_specs=placed,
        out_specs=(
            P(("dp", "expert"), None),
            P(("dp", "expert"), None),
            P("expert", "dp", None),
            P("expert", "dp", None),
            P("expert", None, "dp"),
        ),
        check_vma=False,
    )
```

```python
import functools

import jax
import jax.numpy as jnp
from jax import lax
from jax.experimental import pallas as pl
from jax.experimental.pallas import tpu as pltpu
from jax.sharding import PartitionSpec as P

CAP = 18
NX, NY, NZ, NC = 4, 4, 8, 2
PLANE = NY * NC
ROWS = NZ * CAP
LAG = 8
MESH = pl.DeviceIdType.MESH
F32 = jnp.float32
BF16 = jnp.bfloat16


def mod(a, n):
    return lax.rem(a + n, n)


class Place:
    def __init__(self):
        self.x = lax.axis_index("dp")
        e = lax.axis_index("expert")
        self.c = lax.rem(e, NC)
        self.z = lax.rem(lax.div(e, NC), NZ)
        self.y = lax.div(e, NC * NZ)
        self.plane = self.y * NC + self.c

    def dev(self, y, z, c):
        return {"expert": (y * NZ + z) * NC + c}

    def at_z(self, step):
        return self.dev(self.y, mod(self.z + step, NZ), self.c)

    def at_y(self, step, c):
        return self.dev(mod(self.y + step, NY), self.z, c)

    def at_x(self, step):
        return {"dp": mod(self.x + step, NX)}

    def peers(self):
        out = [self.at_z(s) for s in range(1, NZ)]
        out += [self.at_y(s, c) for s in (1, -1) for c in range(NC)]
        out += [self.at_y(0, 1 - self.c), self.at_x(1), self.at_x(-1)]
        return out


def greet(me):
    barrier = pltpu.get_barrier_semaphore()
    peers = me.peers()
    for peer in peers:
        pl.semaphore_signal(barrier, inc=1, device_id=peer, device_id_type=MESH)
    pl.semaphore_wait(barrier, len(peers))


def remote(src, dst, send, recv, dev):
    return pltpu.make_async_remote_copy(
        src_ref=src, dst_ref=dst, send_sem=send, recv_sem=recv, device_id=dev, device_id_type=MESH
    )


def plane_send(me, piece, landing, relay, send, recv, relay_recv):
    for step, core in ((1, 0), (-1, 1)):
        remote(
            piece(mod(me.y + 2, NY) * NC + core), relay(core), send, relay_recv(core), me.at_y(step, me.c)
        ).start()
    for step in (1, -1):
        for core in range(NC):
            there = mod(me.y + step, NY)
            remote(piece(there * NC + core), landing(me.plane), send, recv, me.at_y(step, core)).start()
    remote(piece(me.y * NC + 1 - me.c), landing(me.plane), send, recv, me.at_y(0, 1 - me.c)).start()


def plane_relay(me, landing, relay, send, recv, relay_recv):
    for step, core in ((1, 0), (-1, 1)):
        remote(relay(core), relay(core), send, relay_recv(core), me.at_y(step, core)).wait_recv()
        origin = mod(me.y - step, NY) * NC + me.c
        remote(relay(core), landing(origin), send, recv, me.at_y(step, core)).start()


def slot_rows(slot_expert, named):
    for z in range(NZ):
        for y in range(NY):
            for c in range(NC):
                at = z * PLANE + y * NC + c
                named[at : at + 1, :] = jnp.full((1, named.shape[1]), slot_expert[(y * NZ + z) * NC + c], jnp.int32)


def dispatch_kernel(
    width,
    chunks,
    tok,
    cot,
    routes,
    probs,
    slots,
    gate,
    up,
    down,
    out_rows,
    out_wide,
    out_grads,
    out_dp,
    key_out,
    zbuf,
    sbuf,
    relay,
    landed,
    wide,
    tall,
    acc,
    racc,
    grads,
    dp,
    pin,
    named,
    maps_own,
    maps,
    pick,
    pbuf,
    prelay,
    own_sem,
    map_send,
    map_recv,
    z_send,
    z_recv,
    y_send,
    y_recv,
    r_recv,
    y_own,
    w_send,
    w_recv,
    w_own,
    out_sem,
):
    me = Place()
    cw = width // chunks
    half = cw // 2
    ff = gate.shape[1]
    depth = gate.shape[0]
    total = 2 * chunks
    rows = tok.shape[0]

    def own_copy(k):
        src = (tok, cot)[k // chunks]
        return pltpu.make_async_copy(
            src.at[:, pl.ds((k % chunks) * cw, cw)], zbuf.at[k, me.z], own_sem.at[k]
        )

    for k in range(total):
        own_copy(k).start()

    hit = jnp.zeros((NZ * PLANE, rows), F32)
    weight = jnp.zeros((NZ * PLANE, rows), F32)
    slot_rows(slots, named)
    turned = routes[...].T
    shares = probs[...].astype(F32).T
    for k in range(turned.shape[0]):
        same = named[...] == turned[k : k + 1, :]
        hit = hit + jnp.where(same, 1.0, 0.0)
        weight = weight + jnp.where(same, shares[k : k + 1, :], 0.0)
    before = lax.broadcasted_iota(jnp.int32, (rows, rows), 0) < lax.broadcasted_iota(
        jnp.int32, (rows, rows), 1
    )
    rank = jnp.dot(
        hit.astype(BF16), jnp.where(before, 1.0, 0.0).astype(BF16), preferred_element_type=F32
    )
    row_of = jnp.where(hit > 0.5, rank + (me.z * CAP).astype(F32), -1.0)
    for z in range(NZ):
        maps_own[z, 0] = row_of[z * PLANE : (z + 1) * PLANE]
        maps_own[z, 1] = weight[z * PLANE : (z + 1) * PLANE]
    maps[me.z] = maps_own[me.z]
    for k in range(total):
        own_copy(k).wait()

    greet(me)

    def z_copy(k, direction, stage):
        sign = 1 - 2 * direction
        block = mod(me.z - sign * stage, NZ)
        if stage == 3:
            where = zbuf.at[k, block, :, pl.ds(direction * half, half)]
        else:
            where = zbuf.at[k, block]
        return remote(
            where, where, z_send.at[k, direction, stage], z_recv.at[k, direction, stage], me.at_z(sign)
        )

    def z_wait(k, direction, stage):
        sign = 1 - 2 * direction
        block = mod(me.z - sign * (stage + 1), NZ)
        if stage == 3:
            where = zbuf.at[k, block, :, pl.ds(direction * half, half)]
        else:
            where = zbuf.at[k, block]
        remote(
            where, where, z_send.at[k, direction, stage], z_recv.at[k, direction, stage], me.at_z(sign)
        ).wait_recv()

    def z_stage(k, stage):
        for direction in (0, 1):
            if stage > 0:
                z_wait(k, direction, stage - 1)
            if stage < 4:
                z_copy(k, direction, stage).start()

    weights = (gate, up, down)

    def w_slot(n, owner):
        if n < 2:
            return wide.at[pl.ds(pl.multiple_of(owner * depth, 128), depth), pl.ds(n * ff, ff)]
        part = down.shape[1]
        return tall.at[:, pl.ds(pl.multiple_of(owner * part, 128), part)]

    def w_copy(n, direction, hop):
        sign = 1 - 2 * direction
        owner = me.x if hop == 0 else mod(me.x - sign, NX)
        src = weights[n] if hop == 0 else w_slot(n, owner)
        return remote(
            src, w_slot(n, owner), w_send.at[n, direction, hop], w_recv.at[n, direction, hop], me.at_x(sign)
        )

    def w_wait(n, direction, hop):
        sign = 1 - 2 * direction
        slot = w_slot(n, mod(me.x - sign * (hop + 1), NX))
        remote(
            slot, slot, w_send.at[n, direction, hop], w_recv.at[n, direction, hop], me.at_x(sign)
        ).wait_recv()

    for s in range(1, NZ):
        z = mod(me.z + s, NZ)
        remote(maps_own.at[z], maps.at[me.z], map_send.at[s], map_recv.at[s], me.at_z(s)).start()
    z_stage(0, 0)
    for n in range(3):
        for direction in (0, 1):
            w_copy(n, direction, 0).start()
        pltpu.make_async_copy(weights[n], w_slot(n, me.x), w_own.at[n]).start()

    for s in range(1, NZ):
        z = mod(me.z - s, NZ)
        remote(maps.at[z], maps.at[z], map_send.at[s], map_recv.at[s], me.at_z(s)).wait_recv()
    row = lax.broadcasted_iota(jnp.int32, (ROWS, rows), 0).astype(F32)
    ones = jnp.ones((rows, rows), BF16)
    for d in range(PLANE):
        share = jnp.zeros((ROWS, rows), F32)
        for z in range(NZ):
            taken = maps[z, 0, d : d + 1, :] == row
            pick[d * ROWS : (d + 1) * ROWS, z * rows : (z + 1) * rows] = jnp.where(taken, 1.0, 0.0).astype(BF16)
            share = share + jnp.where(taken, maps[z, 1, d : d + 1, :], 0.0)
            key_out[d : d + 1, z * rows : (z + 1) * rows] = maps[z, 0, d : d + 1, :]
        pbuf[d] = jnp.dot(share.astype(BF16), ones, preferred_element_type=F32).astype(BF16)

    last = total

    def piece(k):
        return lambda d: sbuf.at[k, d]

    def relay_of(k):
        return lambda core: relay.at[k, core]

    def relay_sem(k):
        return lambda core: r_recv.at[k, core]

    def landing(k):
        return lambda slot: landed.at[k, slot]

    def own_rows(k):
        return pltpu.make_async_copy(sbuf.at[k, me.plane], landed.at[k, me.plane], y_own.at[k])

    def send_chunk(k):
        plane_send(me, piece(k), landing(k), relay_of(k), y_send.at[k], y_recv.at[k], relay_sem(k))
        own_rows(k).start()

    def relay_chunk(k):
        plane_relay(me, landing(k), relay_of(k), y_send.at[k], y_recv.at[k], relay_sem(k))

    def seven_of(k):
        sent, here = sbuf.at[k, pl.ds(0, PLANE - 1)], landed.at[k, pl.ds(0, PLANE - 1)]
        return remote(sent, here, y_send.at[k], y_recv.at[k], me.at_y(1, 0))

    def rows_out(k):
        return pltpu.make_async_copy(landed.at[k], out_rows.at[k], out_sem.at[k])

    def consume(k):
        seven_of(k).wait_recv()
        own_rows(k).wait()

        @pl.when(k < chunks)
        def _():
            take = pl.ds(pl.multiple_of(k * cw, cw), cw)
            acc[...] += jnp.dot(
                landed[k].reshape(PLANE * ROWS, cw), wide[take, :], preferred_element_type=F32
            )

        @pl.when(k >= chunks)
        def _():
            take = pl.ds(pl.multiple_of((k - chunks) * cw, cw), cw)
            racc[...] += lax.dot_general(
                landed[k].reshape(PLANE * ROWS, cw),
                tall[:, take],
                (((1,), (1,)), ((), ())),
                preferred_element_type=F32,
            )
            for d in range(PLANE):
                for j in range(cw // rows):
                    part = slice(j * rows, (j + 1) * rows)
                    scaled = landed[k, d, :, part].astype(F32) * pin[d].astype(F32)
                    landed[k, d, :, part] = scaled.astype(BF16)

        rows_out(k).start()

    def p_land(slot):
        return pin.at[slot]

    def p_relay(core):
        return prelay.at[core]

    def p_sem(core):
        return r_recv.at[last, core]

    acc[...] = jnp.zeros_like(acc)
    racc[...] = jnp.zeros_like(racc)

    def wide_out(n):
        if n == 0:
            return pltpu.make_async_copy(wide, out_wide, out_sem.at[total])
        return pltpu.make_async_copy(grads, out_grads, out_sem.at[total + 1])

    def p_seven():
        sent, here = pbuf.at[pl.ds(0, PLANE - 1)], pin.at[pl.ds(0, PLANE - 1)]
        return remote(sent, here, y_send.at[last], y_recv.at[last], me.at_y(1, 0))

    def step(i, carry):
        @pl.when((i >= 1) & (i < total))
        def _():
            z_stage(i, 0)

        for stage in (1, 2, 3):

            @pl.when((i >= stage) & (i < total + stage))
            def _(stage=stage):
                z_stage(i - stage, stage)

        @pl.when((i >= 4) & (i < total + 4))
        def _():
            k = i - 4
            z_stage(k, 4)
            block = zbuf[k].reshape(NZ * rows, cw)
            out = jnp.dot(pick[...], block, preferred_element_type=F32).astype(BF16)
            sbuf[k] = out.reshape(PLANE, ROWS, cw)
            send_chunk(k)

        @pl.when((i >= 6) & (i < total + 6))
        def _():
            relay_chunk(i - 6)

        @pl.when(i == 5)
        def _():
            for n in range(3):
                for direction in (0, 1):
                    w_wait(n, direction, 0)
                w_copy(n, 0 if n < 2 else 1, 1).start()

        @pl.when(i == 6)
        def _():
            plane_send(me, lambda d: pbuf.at[d], p_land, p_relay, y_send.at[last], y_recv.at[last], p_sem)
            pltpu.make_async_copy(pbuf.at[me.plane], pin.at[me.plane], y_own.at[last]).start()

        @pl.when(i == 8)
        def _():
            plane_relay(me, p_land, p_relay, y_send.at[last], y_recv.at[last], p_sem)

        @pl.when(i == LAG)
        def _():
            for n in range(3):
                w_wait(n, 0 if n < 2 else 1, 1)
                pltpu.make_async_copy(weights[n], w_slot(n, me.x), w_own.at[n]).wait()
            wide_out(0).start()

        @pl.when(i == chunks + LAG)
        def _():
            p_seven().wait_recv()
            pltpu.make_async_copy(pbuf.at[me.plane], pin.at[me.plane], y_own.at[last]).wait()

        @pl.when((i >= LAG) & (i < total + LAG))
        def _():
            consume(i - LAG)

        return carry

    lax.fori_loop(0, total + LAG, step, 0)

    def point(d, carry):
        these = pl.ds(pl.multiple_of(d * ROWS, 16), ROWS)
        g, u, r = acc[these, :ff], acc[these, ff:], racc[these, :]
        p = pin[d].astype(F32)
        p = jnp.concatenate([p] * (ff // rows), axis=1)
        sg = jax.nn.sigmoid(g)
        act = g * sg
        hidden = (act * u).astype(BF16)
        given = jnp.sum(hidden.astype(F32) * r, axis=1, keepdims=True)
        dp[d] = jnp.broadcast_to(given, (ROWS, rows)).astype(BF16)
        dh = p * r
        grads[these, :ff] = (dh * u * sg * (1.0 + g * (1.0 - sg))).astype(BF16)
        grads[these, ff : 2 * ff] = (dh * act).astype(BF16)
        grads[these, 2 * ff :] = hidden
        return carry

    lax.fori_loop(0, PLANE, point, 0)
    dp_out = pltpu.make_async_copy(dp, out_dp, out_sem.at[total + 2])
    wide_out(1).start()
    dp_out.start()

    for n in range(3):
        for direction in (0, 1):
            w_copy(n, direction, 0).wait_send()
        w_copy(n, 0 if n < 2 else 1, 1).wait_send()
    for s in range(1, NZ):
        z = mod(me.z + s, NZ)
        remote(maps_own.at[z], maps.at[me.z], map_send.at[s], map_recv.at[s], me.at_z(s)).wait_send()

    def drain(k, carry):
        for direction in (0, 1):
            for stage in range(4):
                z_copy(k, direction, stage).wait_send()
        seven_of(k).wait_send()
        two = sbuf.at[k, pl.ds(0, 2)]
        remote(two, two, y_send.at[k], y_recv.at[k], me.at_y(1, 0)).wait_send()
        rows_out(k).wait()
        return carry

    lax.fori_loop(0, total, drain, 0)
    two = pbuf.at[pl.ds(0, 2)]
    p_seven().wait_send()
    remote(two, two, y_send.at[last], y_recv.at[last], me.at_y(1, 0)).wait_send()
    wide_out(0).wait()
    wide_out(1).wait()
    dp_out.wait()


def dispatch(tokens, cotangent, routes, probs, slots, gate, up, down, chunks=8):
    rows, width = tokens.shape
    depth, ff = gate.shape
    cw, total = width // chunks, 2 * chunks
    dma = pltpu.SemaphoreType.DMA
    vmem = pl.BlockSpec(memory_space=pltpu.VMEM)
    anyp = pl.BlockSpec(memory_space=pl.ANY)
    shape = jax.ShapeDtypeStruct
    return pl.pallas_call(
        functools.partial(dispatch_kernel, width, chunks),
        out_shape=(
            shape((total, PLANE, ROWS, cw), BF16),
            shape((NX * depth, 2 * ff), BF16),
            shape((PLANE * ROWS, 3 * ff), BF16),
            shape((PLANE, ROWS, rows), BF16),
            shape((PLANE, NZ * rows), F32),
        ),
        in_specs=[anyp, anyp, vmem, vmem, pl.BlockSpec(memory_space=pltpu.SMEM), vmem, vmem, vmem],
        out_specs=(anyp, anyp, anyp, anyp, vmem),
        scratch_shapes=[
            pltpu.VMEM((total, NZ, rows, cw), BF16),
            pltpu.VMEM((total, PLANE, ROWS, cw), BF16),
            pltpu.VMEM((total, 2, ROWS, cw), BF16),
            pltpu.VMEM((total, PLANE, ROWS, cw), BF16),
            pltpu.VMEM((NX * depth, 2 * ff), BF16),
            pltpu.VMEM((ff, width), BF16),
            pltpu.VMEM((PLANE * ROWS, 2 * ff), F32),
            pltpu.VMEM((PLANE * ROWS, ff), F32),
            pltpu.VMEM((PLANE * ROWS, 3 * ff), BF16),
            pltpu.VMEM((PLANE, ROWS, rows), BF16),
            pltpu.VMEM((PLANE, ROWS, rows), BF16),
            pltpu.VMEM((NZ * PLANE, rows), jnp.int32),
            pltpu.VMEM((NZ, 2, PLANE, rows), F32),
            pltpu.VMEM((NZ, 2, PLANE, rows), F32),
            pltpu.VMEM((PLANE * ROWS, NZ * rows), BF16),
            pltpu.VMEM((PLANE, ROWS, rows), BF16),
            pltpu.VMEM((2, ROWS, rows), BF16),
            dma((total,)),
            dma((NZ,)),
            dma((NZ,)),
            dma((total, 2, 4)),
            dma((total, 2, 4)),
            dma((total + 1,)),
            dma((total + 1,)),
            dma((total + 1, 2)),
            dma((total + 1,)),
            dma((3, 2, 2)),
            dma((3, 2, 2)),
            dma((3,)),
            dma((total + 3,)),
        ],
        compiler_params=pltpu.CompilerParams(
            collective_id=0, has_side_effects=True, vmem_limit_bytes=60 * 1024 * 1024
        ),
        name="dispatch",
    )(tokens, cotangent, routes, probs, slots, gate, up, down)


def combine_kernel(
    width,
    chunks,
    rows_in,
    wide_in,
    grads_in,
    dp,
    key,
    routes,
    slots,
    out_tok,
    out_prob,
    out_gate,
    out_up,
    out_down,
    rbuf,
    relay,
    spread,
    gbuf,
    zout,
    zin,
    pbuf,
    prelay,
    maps_own,
    maps,
    kept,
    wide,
    grads,
    dx,
    named,
    wmid0,
    wmid1,
    wmid2,
    wout0,
    wout1,
    wout2,
    win0,
    win1,
    win2,
    map_send,
    map_recv,
    z_send,
    z_recv,
    y_send,
    y_recv,
    r_recv,
    y_own,
    w_send,
    w_recv,
    load_sem,
):
    me = Place()
    cw = width // chunks
    half = cw // 2
    ff = out_gate.shape[1]
    per = width // NX // cw
    rows = out_tok.shape[0]
    last = chunks
    parts = ((wmid0, wout0, win0, out_gate), (wmid1, wout1, win1, out_up), (wmid2, wout2, win2, out_down))
    way = (1, -1, 1)

    def load(n):
        if n < chunks:
            take = pl.ds(n * cw, cw)
            return pltpu.make_async_copy(wide_in.at[take], wide.at[take], load_sem.at[n])
        if n == chunks:
            return pltpu.make_async_copy(grads_in, grads, load_sem.at[n])
        return pltpu.make_async_copy(rows_in, kept, load_sem.at[n])

    load(chunks).start()
    for n in range(chunks):
        load(n).start()
    load(chunks + 1).start()
    slot_rows(slots, named)

    lane = lax.broadcasted_iota(jnp.int32, (NZ * rows, 128), 1).astype(F32)
    turned = key[...].T
    for j in range(PLANE * ROWS // 128):
        tile = jnp.zeros((NZ * rows, 128), F32)
        for d in range(128 * j // ROWS, (128 * j + 127) // ROWS + 1):
            mine = turned[:, d : d + 1]
            where = jnp.where(mine >= 0.0, mine + float(d * ROWS - 128 * j), -1.0)
            tile = tile + jnp.where(where == lane, 1.0, 0.0)
        spread[:, j * 128 : (j + 1) * 128] = tile.astype(BF16)

    greet(me)

    def cols(k):
        return pl.ds(pl.multiple_of(k * cw, cw), cw)

    def piece(k):
        return lambda d: dx.at[k, d]

    def landing(k):
        return lambda slot: rbuf.at[k, slot]

    def relay_of(k):
        return lambda core: relay.at[k, core]

    def relay_sem(k):
        return lambda core: r_recv.at[k, core]

    def y_start(k):
        out = lax.dot_general(
            grads[:, : 2 * ff], wide[cols(k), :], (((1,), (1,)), ((), ())), preferred_element_type=F32
        )
        dx[k] = out.astype(BF16).reshape(PLANE, ROWS, cw)
        plane_send(me, piece(k), landing(k), relay_of(k), y_send.at[k], y_recv.at[k], relay_sem(k))
        pltpu.make_async_copy(piece(k)(me.plane), rbuf.at[k, me.plane], y_own.at[k]).start()

    def y_pass(k):
        plane_relay(me, landing(k), relay_of(k), y_send.at[k], y_recv.at[k], relay_sem(k))

    def p_land(slot):
        return pbuf.at[slot]

    def p_relay(core):
        return prelay.at[core]

    def p_sem(core):
        return r_recv.at[last, core]

    plane_send(me, lambda d: dp.at[d], p_land, p_relay, y_send.at[last], y_recv.at[last], p_sem)
    pltpu.make_async_copy(dp.at[me.plane], pbuf.at[me.plane], y_own.at[last]).start()
    load(chunks).wait()
    for n in range(chunks):
        load(n).wait()
    y_start(0)
    y_start(1)
    plane_relay(me, p_land, p_relay, y_send.at[last], y_recv.at[last], p_sem)

    def w_copy(n, hop):
        sign = way[n] if hop < 2 else -way[n]
        return remote(
            parts[n][1].at[hop], parts[n][2].at[hop], w_send.at[n, hop], w_recv.at[n, hop], me.at_x(sign)
        )

    def put(n, off, j, value):
        where = (slice(j * cw, (j + 1) * cw), slice(None))
        if n == 2:
            where = where[::-1]
        if off == 0:
            parts[n][3][where] = value
        elif off == way[n]:
            parts[n][0][where] = value
        else:
            parts[n][1][(0 if off == 2 else 2,) + where] = value.astype(BF16)

    def w_block(off):
        owner = mod(me.x + off, NX)
        down_to = (((0,), (0,)), ((), ()))
        for j in range(per):
            x = kept[owner * per + j].reshape(PLANE * ROWS, cw)
            w = kept[chunks + owner * per + j].reshape(PLANE * ROWS, cw)
            both = lax.dot_general(x, grads[:, : 2 * ff], down_to, preferred_element_type=F32)
            put(0, off, j, both[:, :ff])
            put(1, off, j, both[:, ff:])
            put(2, off, j, lax.dot_general(grads[:, 2 * ff :], w, down_to, preferred_element_type=F32))

    def w_second():
        for n in range(3):
            w_copy(n, 0).wait_recv()
            summed = parts[n][0][...] + parts[n][2][0].astype(F32)
            parts[n][1][1] = summed.astype(BF16)
        for n in range(3):
            w_copy(n, 1).start()

    def w_third():
        for n in range(3):
            w_copy(n, 1).wait_recv()
            w_copy(n, 2).wait_recv()
            parts[n][3][...] += parts[n][2][1].astype(F32) + parts[n][2][2].astype(F32)

    def w_work(i):
        @pl.when(i == 0)
        def _():
            load(chunks + 1).wait()
            w_block(2)
            for n in range(3):
                w_copy(n, 0).start()

        @pl.when(i == 1)
        def _():
            w_block(1)
            w_copy(1, 2).start()

        @pl.when(i == 2)
        def _():
            w_block(-1)
            w_copy(0, 2).start()
            w_copy(2, 2).start()

        @pl.when(i == 4)
        def _():
            w_second()

        @pl.when(i == 6)
        def _():
            w_block(0)

    def z_copy(k, direction, stage):
        sign = 1 - 2 * direction
        if stage == 0:
            part = pl.ds(direction * half, half)
            src, dst = zout.at[k, direction, 0, :, part], zin.at[k, direction, 0, :, part]
        else:
            src, dst = zout.at[k, direction, stage], zin.at[k, direction, stage]
        return remote(src, dst, z_send.at[k, direction, stage], z_recv.at[k, direction, stage], me.at_z(sign))

    def z_stage(k, stage):
        for direction in (0, 1):
            sign = 1 - 2 * direction
            block = mod(me.z + sign * (4 - stage), NZ)
            if stage == 0:
                part = slice(direction * half, (direction + 1) * half)
                zout[k, direction, 0, :, part] = gbuf[k, block, :, part].astype(BF16)
            else:
                z_copy(k, direction, stage - 1).wait_recv()
                if stage == 1:
                    near = slice(direction * half, (direction + 1) * half)
                    rest = slice((1 - direction) * half, (2 - direction) * half)
                    summed = gbuf[k, block, :, near] + zin[k, direction, 0, :, near].astype(F32)
                    zout[k, direction, 1, :, near] = summed.astype(BF16)
                    zout[k, direction, 1, :, rest] = gbuf[k, block, :, rest].astype(BF16)
                else:
                    summed = gbuf[k, block] + zin[k, direction, stage - 1].astype(F32)
                    zout[k, direction, stage] = summed.astype(BF16)
            z_copy(k, direction, stage).start()

    def z_finish(k):
        z_copy(k, 0, 3).wait_recv()
        z_copy(k, 1, 3).wait_recv()
        summed = gbuf[k, me.z] + zin[k, 0, 3].astype(F32) + zin[k, 1, 3].astype(F32)
        out_tok[:, cols(k)] = summed.astype(BF16)

    def y_wait(k):
        seven = rbuf.at[k, pl.ds(0, PLANE - 1)]
        remote(seven, seven, y_send.at[k], y_recv.at[k], me.at_y(1, 0)).wait_recv()
        pltpu.make_async_copy(piece(k)(me.plane), rbuf.at[k, me.plane], y_own.at[k]).wait()

    def map_copy(s):
        z = mod(me.z + s, NZ)
        return remote(maps_own.at[z], maps.at[me.z], map_send.at[s], map_recv.at[s], me.at_z(s))

    def prob_grads():
        seven = pbuf.at[pl.ds(0, PLANE - 1)]
        remote(seven, seven, y_send.at[last], y_recv.at[last], me.at_y(1, 0)).wait_recv()
        pltpu.make_async_copy(dp.at[me.plane], pbuf.at[me.plane], y_own.at[last]).wait()
        row = lax.broadcasted_iota(jnp.int32, (ROWS, rows), 0).astype(F32)
        for d in range(PLANE):
            given = pbuf[d].astype(F32)
            for z in range(NZ):
                taken = key[d : d + 1, z * rows : (z + 1) * rows] == row
                maps_own[z, d : d + 1, :] = jnp.sum(jnp.where(taken, given, 0.0), axis=0, keepdims=True)
        maps[me.z] = maps_own[me.z]
        for s in range(1, NZ):
            map_copy(s).start()

    def step(i, carry):
        @pl.when(i + 2 < chunks)
        def _():
            y_start(i + 2)

        @pl.when((i >= 1) & (i <= chunks))
        def _():
            y_pass(i - 1)

        for stage in (1, 2, 3):

            @pl.when((i >= 2 + stage) & (i < chunks + 2 + stage))
            def _(stage=stage):
                z_stage(i - 2 - stage, stage)

        @pl.when((i >= 2) & (i <= chunks + 1))
        def _():
            k = i - 2
            y_wait(k)
            got = rbuf[k].reshape(PLANE * ROWS, cw)
            gbuf[k] = jnp.dot(spread[...], got, preferred_element_type=F32).reshape(NZ, rows, cw)
            z_stage(k, 0)

        @pl.when((i >= 6) & (i < chunks + 6))
        def _():
            z_finish(i - 6)

        @pl.when(i == 3)
        def _():
            prob_grads()

        w_work(i)
        return carry

    lax.fori_loop(0, chunks + 6, step, 0)
    w_third()
    for s in range(1, NZ):
        z = mod(me.z - s, NZ)
        remote(maps.at[z], maps.at[z], map_send.at[s], map_recv.at[s], me.at_z(s)).wait_recv()
    given = maps[...].reshape(NZ * PLANE, rows)
    wanted = routes[...].T
    for k in range(wanted.shape[0]):
        same = named[...] == wanted[k : k + 1, :]
        out_prob[k : k + 1, :] = jnp.sum(jnp.where(same, given, 0.0), axis=0, keepdims=True)

    def drain(k, carry):
        for direction in (0, 1):
            for stage in range(4):
                z_copy(k, direction, stage).wait_send()
        seven, two = rbuf.at[k, pl.ds(0, PLANE - 1)], rbuf.at[k, pl.ds(0, 2)]
        remote(seven, seven, y_send.at[k], y_recv.at[k], me.at_y(1, 0)).wait_send()
        remote(two, two, y_send.at[k], y_recv.at[k], me.at_y(1, 0)).wait_send()
        return carry

    lax.fori_loop(0, chunks, drain, 0)
    seven, two = pbuf.at[pl.ds(0, PLANE - 1)], pbuf.at[pl.ds(0, 2)]
    remote(seven, seven, y_send.at[last], y_recv.at[last], me.at_y(1, 0)).wait_send()
    remote(two, two, y_send.at[last], y_recv.at[last], me.at_y(1, 0)).wait_send()
    for s in range(1, NZ):
        map_copy(s).wait_send()
    for n in range(3):
        for hop in range(3):
            w_copy(n, hop).wait_send()


def combine(rows_in, wide, grads, dp, key, routes, slots):
    total, _, _, cw = rows_in.shape
    chunks = total // 2
    width = chunks * cw
    rows = dp.shape[2]
    depth, ff = wide.shape[0] // NX, wide.shape[1] // 2
    dma = pltpu.SemaphoreType.DMA
    vmem = pl.BlockSpec(memory_space=pltpu.VMEM)
    smem = pl.BlockSpec(memory_space=pltpu.SMEM)
    anyp = pl.BlockSpec(memory_space=pl.ANY)
    shape = jax.ShapeDtypeStruct
    one, two = (depth, ff), (ff, width // NX)
    return pl.pallas_call(
        functools.partial(combine_kernel, width, chunks),
        out_shape=(
            shape((rows, width), BF16),
            shape(routes.shape[::-1], F32),
            shape(one, F32),
            shape(one, F32),
            shape(two, F32),
        ),
        in_specs=[anyp, anyp, anyp, anyp, vmem, vmem, smem],
        out_specs=(vmem, vmem, vmem, vmem, vmem),
        scratch_shapes=[
            pltpu.VMEM((chunks, PLANE, ROWS, cw), BF16),
            pltpu.VMEM((chunks, 2, ROWS, cw), BF16),
            pltpu.VMEM((NZ * rows, PLANE * ROWS), BF16),
            pltpu.VMEM((chunks, NZ, rows, cw), F32),
            pltpu.VMEM((chunks, 2, 4, rows, cw), BF16),
            pltpu.VMEM((chunks, 2, 4, rows, cw), BF16),
            pltpu.VMEM((PLANE, ROWS, rows), BF16),
            pltpu.VMEM((2, ROWS, rows), BF16),
            pltpu.VMEM((NZ, PLANE, rows), F32),
            pltpu.VMEM((NZ, PLANE, rows), F32),
            pltpu.VMEM(rows_in.shape, BF16),
            pltpu.VMEM(wide.shape, BF16),
            pltpu.VMEM(grads.shape, BF16),
            pltpu.VMEM((chunks, PLANE, ROWS, cw), BF16),
            pltpu.VMEM((NZ * PLANE, rows), jnp.int32),
            pltpu.VMEM(one, F32),
            pltpu.VMEM(one, F32),
            pltpu.VMEM(two, F32),
            pltpu.VMEM((3,) + one, BF16),
            pltpu.VMEM((3,) + one, BF16),
            pltpu.VMEM((3,) + two, BF16),
            pltpu.VMEM((3,) + one, BF16),
            pltpu.VMEM((3,) + one, BF16),
            pltpu.VMEM((3,) + two, BF16),
            dma((NZ,)),
            dma((NZ,)),
            dma((chunks, 2, 4)),
            dma((chunks, 2, 4)),
            dma((chunks + 1,)),
            dma((chunks + 1,)),
            dma((chunks + 1, 2)),
            dma((chunks + 1,)),
            dma((3, 3)),
            dma((3, 3)),
            dma((chunks + 2,)),
        ],
        compiler_params=pltpu.CompilerParams(
            collective_id=1, has_side_effects=True, vmem_limit_bytes=67043328
        ),
        name="combine",
    )(rows_in, wide, grads, dp, key, routes, slots)


def shards(tokens, cotangent, routes, probs, slot_expert, gate_w, up_w, down_w):
    rows_in, wide, grads, dp, key = dispatch(
        tokens, cotangent, routes, probs, slot_expert, gate_w[0], up_w[0], down_w[0]
    )
    grad_tokens, grad_probs, grad_gate, grad_up, grad_down = combine(
        rows_in, wide, grads, dp, key, routes, slot_expert
    )
    return (
        grad_tokens,
        grad_probs.T.astype(BF16),
        grad_gate[None],
        grad_up[None],
        grad_down[None],
    )


def solution(mesh):
    placed = (
        P(("dp", "expert"), None),
        P(("dp", "expert"), None),
        P(("dp", "expert"), None),
        P(("dp", "expert"), None),
        P(),
        P("expert", "dp", None),
        P("expert", "dp", None),
        P("expert", None, "dp"),
    )
    return jax.shard_map(
        shards,
        mesh=mesh,
        in_specs=placed,
        out_specs=(
            P(("dp", "expert"), None),
            P(("dp", "expert"), None),
            P("expert", "dp", None),
            P("expert", "dp", None),
            P("expert", None, "dp"),
        ),
        check_vma=False,
    )
```

```python
import functools

import jax
import jax.numpy as jnp
from jax import lax
from jax.experimental import pallas as pl
from jax.experimental.pallas import tpu as pltpu
from jax.sharding import PartitionSpec as P

CAP = 18
NX, NY, NZ, NC = 4, 4, 8, 2
PLANE = NY * NC
ROWS = NZ * CAP
LAG = 8
W_PASS = 9
W_USE = 14
MESH = pl.DeviceIdType.MESH
F32 = jnp.float32
BF16 = jnp.bfloat16


def mod(a, n):
    return lax.rem(a + n, n)


class Place:
    def __init__(self):
        self.x = lax.axis_index("dp")
        e = lax.axis_index("expert")
        self.c = lax.rem(e, NC)
        self.z = lax.rem(lax.div(e, NC), NZ)
        self.y = lax.div(e, NC * NZ)
        self.plane = self.y * NC + self.c

    def dev(self, y, z, c):
        return {"expert": (y * NZ + z) * NC + c}

    def at_z(self, step):
        return self.dev(self.y, mod(self.z + step, NZ), self.c)

    def at_y(self, step, c):
        return self.dev(mod(self.y + step, NY), self.z, c)

    def at_x(self, step):
        return {"dp": mod(self.x + step, NX)}

    def peers(self):
        out = [self.at_z(s) for s in range(1, NZ)]
        out += [self.at_y(s, c) for s in (1, 2, 3) for c in range(NC)]
        out += [self.at_y(0, 1 - self.c), self.at_x(1), self.at_x(-1)]
        return out


def hail(me):
    for peer in me.peers():
        pl.semaphore_signal(pltpu.get_barrier_semaphore(), inc=1, device_id=peer, device_id_type=MESH)


def met(me):
    pl.semaphore_wait(pltpu.get_barrier_semaphore(), len(me.peers()))


def diagonal(count, lanes):
    down = lax.broadcasted_iota(jnp.int32, (count, lanes), 0)
    return down == lax.broadcasted_iota(jnp.int32, (count, lanes), 1)


def fold(column, lanes):
    rest = ROWS - lanes
    first = jnp.sum(jnp.where(diagonal(lanes, lanes), column[:lanes], 0.0), axis=0, keepdims=True)
    second = jnp.sum(jnp.where(diagonal(rest, lanes), column[lanes:], 0.0), axis=0, keepdims=True)
    return jnp.concatenate([first, second, jnp.zeros((6, lanes), F32)], axis=0)


def unfold(tile):
    lanes = tile.shape[1]
    first = jnp.sum(jnp.where(diagonal(lanes, lanes), tile[0:1], 0.0), axis=1, keepdims=True)
    second = jnp.sum(jnp.where(diagonal(ROWS - lanes, lanes), tile[1:2], 0.0), axis=1, keepdims=True)
    return jnp.broadcast_to(jnp.concatenate([first, second], axis=0), (ROWS, lanes))


def remote(src, dst, send, recv, dev):
    return pltpu.make_async_remote_copy(
        src_ref=src, dst_ref=dst, send_sem=send, recv_sem=recv, device_id=dev, device_id_type=MESH
    )


def plane_send(me, piece, landing, send, recv):
    for step in (2, 1, -1):
        for core in range(NC):
            there = mod(me.y + step, NY)
            remote(piece(there * NC + core), landing(me.plane), send, recv, me.at_y(step, core)).start()
    remote(piece(me.y * NC + 1 - me.c), landing(me.plane), send, recv, me.at_y(0, 1 - me.c)).start()


def slot_rows(slot_expert, named):
    for z in range(NZ):
        for y in range(NY):
            for c in range(NC):
                at = z * PLANE + y * NC + c
                named[at : at + 1, :] = jnp.full((1, named.shape[1]), slot_expert[(y * NZ + z) * NC + c], jnp.int32)


def dispatch_kernel(
    width,
    chunks,
    tok,
    cot,
    routes,
    probs,
    slots,
    gate,
    up,
    down,
    out_rows,
    out_wide,
    out_grads,
    out_dp,
    key_out,
    zbuf,
    sbuf,
    landed,
    wide,
    tall,
    acc,
    racc,
    grads,
    dp,
    pin,
    share_of,
    named,
    maps_own,
    maps,
    pick,
    pbuf,
    own_sem,
    map_send,
    map_recv,
    z_send,
    z_recv,
    y_send,
    y_recv,
    y_own,
    w_send,
    w_recv,
    w_own,
    out_sem,
):
    me = Place()
    cw = width // chunks
    half = cw // 2
    ff = gate.shape[1]
    depth = gate.shape[0]
    total = 2 * chunks
    rows = tok.shape[0]

    hail(me)

    def own_copy(k):
        src = (tok, cot)[k // chunks]
        return pltpu.make_async_copy(
            src.at[:, pl.ds((k % chunks) * cw, cw)], zbuf.at[k, me.z], own_sem.at[k]
        )

    for k in range(total):
        own_copy(k).start()

    hit = jnp.zeros((NZ * PLANE, rows), F32)
    weight = jnp.zeros((NZ * PLANE, rows), F32)
    slot_rows(slots, named)
    turned = routes[...]
    shares = probs[...].astype(F32)
    for k in range(turned.shape[0]):
        same = named[...] == turned[k : k + 1, :]
        hit = hit + jnp.where(same, 1.0, 0.0)
        weight = weight + jnp.where(same, shares[k : k + 1, :], 0.0)
    before = lax.broadcasted_iota(jnp.int32, (rows, rows), 0) < lax.broadcasted_iota(
        jnp.int32, (rows, rows), 1
    )
    rank = jnp.dot(
        hit.astype(BF16), jnp.where(before, 1.0, 0.0).astype(BF16), preferred_element_type=F32
    )
    row_of = jnp.where(hit > 0.5, rank + (me.z * CAP).astype(F32), -1.0)
    for z in range(NZ):
        maps_own[z, 0] = row_of[z * PLANE : (z + 1) * PLANE]
        maps_own[z, 1] = weight[z * PLANE : (z + 1) * PLANE]
    maps[me.z] = maps_own[me.z]
    for k in range(total):
        own_copy(k).wait()

    met(me)

    def z_copy(k, direction, stage):
        sign = 1 - 2 * direction
        block = mod(me.z - sign * stage, NZ)
        if stage == 3:
            where = zbuf.at[k, block, :, pl.ds(direction * half, half)]
        else:
            where = zbuf.at[k, block]
        return remote(
            where, where, z_send.at[k, direction, stage], z_recv.at[k, direction, stage], me.at_z(sign)
        )

    def z_wait(k, direction, stage):
        sign = 1 - 2 * direction
        block = mod(me.z - sign * (stage + 1), NZ)
        if stage == 3:
            where = zbuf.at[k, block, :, pl.ds(direction * half, half)]
        else:
            where = zbuf.at[k, block]
        remote(
            where, where, z_send.at[k, direction, stage], z_recv.at[k, direction, stage], me.at_z(sign)
        ).wait_recv()

    def z_stage(k, stage):
        for direction in (0, 1):
            if stage > 0:
                z_wait(k, direction, stage - 1)
            if stage < 4:
                z_copy(k, direction, stage).start()

    weights = (gate, up, down)

    def w_slot(n, owner):
        if n < 2:
            return wide.at[pl.ds(pl.multiple_of(owner * depth, 128), depth), pl.ds(n * ff, ff)]
        part = down.shape[1]
        return tall.at[:, pl.ds(pl.multiple_of(owner * part, 128), part)]

    def w_copy(n, direction, hop):
        sign = 1 - 2 * direction
        owner = me.x if hop == 0 else mod(me.x - sign, NX)
        src = weights[n] if hop == 0 else w_slot(n, owner)
        return remote(
            src, w_slot(n, owner), w_send.at[n, direction, hop], w_recv.at[n, direction, hop], me.at_x(sign)
        )

    def w_wait(n, direction, hop):
        sign = 1 - 2 * direction
        slot = w_slot(n, mod(me.x - sign * (hop + 1), NX))
        remote(
            slot, slot, w_send.at[n, direction, hop], w_recv.at[n, direction, hop], me.at_x(sign)
        ).wait_recv()

    for s in range(1, NZ):
        z = mod(me.z + s, NZ)
        remote(maps_own.at[z], maps.at[me.z], map_send.at[s], map_recv.at[s], me.at_z(s)).start()
    z_stage(0, 0)
    for n in range(3):
        for direction in (0, 1):
            w_copy(n, direction, 0).start()
        pltpu.make_async_copy(weights[n], w_slot(n, me.x), w_own.at[n]).start()

    def choose(d):
        row = lax.broadcasted_iota(jnp.int32, (ROWS, rows), 0).astype(F32)
        share = jnp.zeros((ROWS, rows), F32)
        for z in range(NZ):
            taken = maps[z, 0, d : d + 1, :] == row
            pick[d * ROWS : (d + 1) * ROWS, z * rows : (z + 1) * rows] = jnp.where(taken, 1.0, 0.0).astype(BF16)
            share = share + jnp.where(taken, maps[z, 1, d : d + 1, :], 0.0)
            key_out[d : d + 1, z * rows : (z + 1) * rows] = maps[z, 0, d : d + 1, :]
        pbuf[d] = fold(jnp.sum(share, axis=1, keepdims=True), rows)

    last = total

    def piece(k):
        return lambda d: sbuf.at[k, d]

    def landing(k):
        return lambda slot: landed.at[k, slot]

    def own_rows(k):
        return pltpu.make_async_copy(sbuf.at[k, me.plane], landed.at[k, me.plane], y_own.at[k])

    def send_chunk(k):
        plane_send(me, piece(k), landing(k), y_send.at[k], y_recv.at[k])
        own_rows(k).start()

    def seven_of(k):
        sent, here = sbuf.at[k, pl.ds(0, PLANE - 1)], landed.at[k, pl.ds(0, PLANE - 1)]
        return remote(sent, here, y_send.at[k], y_recv.at[k], me.at_y(1, 0))

    def rows_out(k):
        return pltpu.make_async_copy(landed.at[k], out_rows.at[k], out_sem.at[k])

    def consume_x(k):
        seven_of(k).wait_recv()
        own_rows(k).wait()
        take = pl.ds(pl.multiple_of(k * cw, cw), cw)
        acc[...] += jnp.dot(landed[k].reshape(PLANE * ROWS, cw), wide[take, :], preferred_element_type=F32)
        rows_out(k).start()

    def consume_dy(k):
        seven_of(k).wait_recv()
        own_rows(k).wait()
        take = pl.ds(pl.multiple_of((k - chunks) * cw, cw), cw)
        racc[...] += lax.dot_general(
            landed[k].reshape(PLANE * ROWS, cw),
            tall[:, take],
            (((1,), (1,)), ((), ())),
            preferred_element_type=F32,
        )
        for d in range(PLANE):
            for j in range(cw // rows):
                part = slice(j * rows, (j + 1) * rows)
                scaled = landed[k, d, :, part].astype(F32) * share_of[d]
                landed[k, d, :, part] = scaled.astype(BF16)
        rows_out(k).start()

    def p_land(slot):
        return pin.at[slot]

    def wide_out(n):
        if n == 0:
            return pltpu.make_async_copy(wide, out_wide, out_sem.at[total])
        return pltpu.make_async_copy(grads, out_grads, out_sem.at[total + 1])

    def p_seven():
        sent, here = pbuf.at[pl.ds(0, PLANE - 1)], pin.at[pl.ds(0, PLANE - 1)]
        return remote(sent, here, y_send.at[last], y_recv.at[last], me.at_y(1, 0))

    def step(i, carry):
        @pl.when((i >= 4) & (i < total + 4))
        def _():
            k = i - 4
            z_stage(k, 4)
            block = zbuf[k].reshape(NZ * rows, cw)
            out = jnp.dot(pick[...], block, preferred_element_type=F32).astype(BF16)
            sbuf[k] = out.reshape(PLANE, ROWS, cw)
            send_chunk(k)

        for stage in (3, 2, 1):

            @pl.when((i >= stage) & (i < total + stage))
            def _(stage=stage):
                z_stage(i - stage, stage)

        @pl.when((i >= 1) & (i < total))
        def _():
            z_stage(i, 0)

        @pl.when(i == 0)
        def _():
            for s in range(1, NZ):
                z = mod(me.z - s, NZ)
                remote(maps.at[z], maps.at[z], map_send.at[s], map_recv.at[s], me.at_z(s)).wait_recv()

        for turn in range(4):

            @pl.when(i == turn)
            def _(turn=turn):
                choose(2 * turn)
                choose(2 * turn + 1)

        @pl.when(i == 6)
        def _():
            acc[...] = jnp.zeros_like(acc)
            racc[...] = jnp.zeros_like(racc)

        @pl.when(i == 4)
        def _():
            plane_send(me, lambda d: pbuf.at[d], p_land, y_send.at[last], y_recv.at[last])
            pltpu.make_async_copy(pbuf.at[me.plane], pin.at[me.plane], y_own.at[last]).start()

        @pl.when(i == W_PASS)
        def _():
            for n in range(3):
                for direction in (0, 1):
                    w_wait(n, direction, 0)
                w_copy(n, 0 if n < 2 else 1, 1).start()

        @pl.when(i == W_USE)
        def _():
            for n in range(3):
                w_wait(n, 0 if n < 2 else 1, 1)
                pltpu.make_async_copy(weights[n], w_slot(n, me.x), w_own.at[n]).wait()
            wide_out(0).start()
            p_seven().wait_recv()
            pltpu.make_async_copy(pbuf.at[me.plane], pin.at[me.plane], y_own.at[last]).wait()
            for d in range(PLANE):
                share_of[d] = unfold(pin[d])

        @pl.when((i >= W_USE) & (i < chunks + W_USE))
        def _():
            consume_x(i - W_USE)

        @pl.when((i >= chunks + LAG) & (i < total + LAG))
        def _():
            consume_dy(i - LAG)

        return carry

    lax.fori_loop(0, total + LAG, step, 0)

    def point(d, carry):
        these = pl.ds(pl.multiple_of(d * ROWS, 16), ROWS)
        g, u, r = acc[these, :ff], acc[these, ff:], racc[these, :]
        p = share_of[d]
        p = jnp.concatenate([p] * (ff // rows), axis=1)
        sg = jax.nn.sigmoid(g)
        act = g * sg
        hidden = (act * u).astype(BF16)
        given = jnp.sum(hidden.astype(F32) * r, axis=1, keepdims=True)
        dp[d] = fold(given.astype(BF16).astype(F32), rows)
        dh = p * r
        grads[these, :ff] = (dh * u * sg * (1.0 + g * (1.0 - sg))).astype(BF16)
        grads[these, ff : 2 * ff] = (dh * act).astype(BF16)
        grads[these, 2 * ff :] = hidden
        return carry

    lax.fori_loop(0, PLANE, point, 0)
    dp_out = pltpu.make_async_copy(dp, out_dp, out_sem.at[total + 2])
    wide_out(1).start()
    dp_out.start()

    for n in range(3):
        for direction in (0, 1):
            w_copy(n, direction, 0).wait_send()
        w_copy(n, 0 if n < 2 else 1, 1).wait_send()
    for s in range(1, NZ):
        z = mod(me.z + s, NZ)
        remote(maps_own.at[z], maps.at[me.z], map_send.at[s], map_recv.at[s], me.at_z(s)).wait_send()

    def drain(k, carry):
        for direction in (0, 1):
            for stage in range(4):
                z_copy(k, direction, stage).wait_send()
        seven_of(k).wait_send()
        rows_out(k).wait()
        return carry

    lax.fori_loop(0, total, drain, 0)
    p_seven().wait_send()
    wide_out(0).wait()
    wide_out(1).wait()
    dp_out.wait()


def dispatch(tokens, cotangent, routes, probs, slots, gate, up, down, chunks=8):
    rows, width = tokens.shape
    depth, ff = gate.shape
    cw, total = width // chunks, 2 * chunks
    dma = pltpu.SemaphoreType.DMA
    vmem = pl.BlockSpec(memory_space=pltpu.VMEM)
    anyp = pl.BlockSpec(memory_space=pl.ANY)
    shape = jax.ShapeDtypeStruct
    return pl.pallas_call(
        functools.partial(dispatch_kernel, width, chunks),
        out_shape=(
            shape((total, PLANE, ROWS, cw), BF16),
            shape((NX * depth, 2 * ff), BF16),
            shape((PLANE * ROWS, 3 * ff), BF16),
            shape((PLANE, 8, rows), F32),
            shape((PLANE, NZ * rows), F32),
        ),
        in_specs=[anyp, anyp, vmem, vmem, pl.BlockSpec(memory_space=pltpu.SMEM), vmem, vmem, vmem],
        out_specs=(anyp, anyp, anyp, anyp, vmem),
        scratch_shapes=[
            pltpu.VMEM((total, NZ, rows, cw), BF16),
            pltpu.VMEM((total, PLANE, ROWS, cw), BF16),
            pltpu.VMEM((total, PLANE, ROWS, cw), BF16),
            pltpu.VMEM((NX * depth, 2 * ff), BF16),
            pltpu.VMEM((ff, width), BF16),
            pltpu.VMEM((PLANE * ROWS, 2 * ff), F32),
            pltpu.VMEM((PLANE * ROWS, ff), F32),
            pltpu.VMEM((PLANE * ROWS, 3 * ff), BF16),
            pltpu.VMEM((PLANE, 8, rows), F32),
            pltpu.VMEM((PLANE, 8, rows), F32),
            pltpu.VMEM((PLANE, ROWS, rows), F32),
            pltpu.VMEM((NZ * PLANE, rows), jnp.int32),
            pltpu.VMEM((NZ, 2, PLANE, rows), F32),
            pltpu.VMEM((NZ, 2, PLANE, rows), F32),
            pltpu.VMEM((PLANE * ROWS, NZ * rows), BF16),
            pltpu.VMEM((PLANE, 8, rows), F32),
            dma((total,)),
            dma((NZ,)),
            dma((NZ,)),
            dma((total, 2, 4)),
            dma((total, 2, 4)),
            dma((total + 1,)),
            dma((total + 1,)),
            dma((total + 1,)),
            dma((3, 2, 2)),
            dma((3, 2, 2)),
            dma((3,)),
            dma((total + 3,)),
        ],
        compiler_params=pltpu.CompilerParams(
            collective_id=0, has_side_effects=True, vmem_limit_bytes=60 * 1024 * 1024
        ),
        name="dispatch",
    )(tokens, cotangent, routes, probs, slots, gate, up, down)


def combine_kernel(
    width,
    chunks,
    rows_in,
    wide_in,
    grads_in,
    dp,
    key,
    routes,
    slots,
    out_tok,
    out_prob,
    out_gate,
    out_up,
    out_down,
    rbuf,
    spread,
    gbuf,
    zout,
    zin,
    pbuf,
    maps_own,
    maps,
    kept,
    wide,
    grads,
    dx,
    named,
    wmid0,
    wmid1,
    wmid2,
    wout0,
    wout1,
    wout2,
    win0,
    win1,
    win2,
    map_send,
    map_recv,
    z_send,
    z_recv,
    y_send,
    y_recv,
    y_own,
    w_send,
    w_recv,
    own0,
    own1,
    own2,
    load_sem,
    w_out,
):
    me = Place()
    cw = width // chunks
    half = cw // 2
    ff = out_gate.shape[1]
    per = width // NX // cw
    rows = out_tok.shape[0]
    last = chunks
    parts = ((wmid0, wout0, win0, own0), (wmid1, wout1, win1, own1), (wmid2, wout2, win2, own2))
    finals = (out_gate, out_up, out_down)
    way = (1, -1, 1)

    def load(n):
        if n < chunks:
            take = pl.ds(n * cw, cw)
            return pltpu.make_async_copy(wide_in.at[take], wide.at[take], load_sem.at[n])
        if n == chunks:
            return pltpu.make_async_copy(grads_in, grads, load_sem.at[n])
        return pltpu.make_async_copy(rows_in, kept, load_sem.at[n])

    hail(me)
    load(chunks).start()
    for n in range(chunks):
        load(n).start()
    load(chunks + 1).start()

    met(me)

    def cols(k):
        return pl.ds(pl.multiple_of(k * cw, cw), cw)

    def piece(k):
        return lambda d: dx.at[k, d]

    def landing(k):
        return lambda slot: rbuf.at[k, slot]

    def y_start(k):
        out = lax.dot_general(
            grads[:, : 2 * ff], wide[cols(k), :], (((1,), (1,)), ((), ())), preferred_element_type=F32
        )
        dx[k] = out.astype(BF16).reshape(PLANE, ROWS, cw)
        plane_send(me, piece(k), landing(k), y_send.at[k], y_recv.at[k])
        pltpu.make_async_copy(piece(k)(me.plane), rbuf.at[k, me.plane], y_own.at[k]).start()

    def p_land(slot):
        return pbuf.at[slot]

    plane_send(me, lambda d: dp.at[d], p_land, y_send.at[last], y_recv.at[last])
    pltpu.make_async_copy(dp.at[me.plane], pbuf.at[me.plane], y_own.at[last]).start()
    load(chunks).wait()
    load(0).wait()
    y_start(0)
    load(1).wait()
    y_start(1)
    for n in range(2, chunks):
        load(n).wait()
    slot_rows(slots, named)

    lane = lax.broadcasted_iota(jnp.int32, (NZ * rows, 128), 1).astype(F32)
    turned = key[...].T
    for j in range(PLANE * ROWS // 128):
        tile = jnp.zeros((NZ * rows, 128), F32)
        for d in range(128 * j // ROWS, (128 * j + 127) // ROWS + 1):
            mine = turned[:, d : d + 1]
            where = jnp.where(mine >= 0.0, mine + float(d * ROWS - 128 * j), -1.0)
            tile = tile + jnp.where(where == lane, 1.0, 0.0)
        spread[:, j * 128 : (j + 1) * 128] = tile.astype(BF16)

    def w_copy(n, hop):
        sign = way[n] if hop < 2 else -way[n]
        return remote(
            parts[n][1].at[hop], parts[n][2].at[hop], w_send.at[n, hop], w_recv.at[n, hop], me.at_x(sign)
        )

    def put(n, off, j, value):
        where = (slice(j * cw, (j + 1) * cw), slice(None))
        if n == 2:
            where = where[::-1]
        if off == 0:
            parts[n][3][where] = value
        elif off == way[n]:
            parts[n][0][where] = value
        else:
            parts[n][1][(0 if off == 2 else 2,) + where] = value.astype(BF16)

    def w_block(off):
        owner = mod(me.x + off, NX)
        down_to = (((0,), (0,)), ((), ()))
        for j in range(per):
            x = kept[owner * per + j].reshape(PLANE * ROWS, cw)
            w = kept[chunks + owner * per + j].reshape(PLANE * ROWS, cw)
            both = lax.dot_general(x, grads[:, : 2 * ff], down_to, preferred_element_type=F32)
            put(0, off, j, both[:, :ff])
            put(1, off, j, both[:, ff:])
            put(2, off, j, lax.dot_general(grads[:, 2 * ff :], w, down_to, preferred_element_type=F32))

    def w_second():
        for n in range(3):
            w_copy(n, 0).wait_recv()
            summed = parts[n][0][...] + parts[n][2][0].astype(F32)
            parts[n][1][1] = summed.astype(BF16)
        for n in range(3):
            w_copy(n, 1).start()

    def w_third():
        for n in range(3):
            w_copy(n, 1).wait_recv()
            w_copy(n, 2).wait_recv()
            parts[n][3][...] += parts[n][2][1].astype(F32) + parts[n][2][2].astype(F32)
            pltpu.make_async_copy(parts[n][3], finals[n], w_out.at[n]).start()

    def w_work(i):
        @pl.when(i == 0)
        def _():
            load(chunks + 1).wait()
            w_block(2)
            for n in range(3):
                w_copy(n, 0).start()

        @pl.when(i == 1)
        def _():
            w_block(1)
            w_copy(1, 2).start()

        @pl.when(i == 2)
        def _():
            w_block(-1)
            w_copy(0, 2).start()
            w_copy(2, 2).start()

        @pl.when(i == 4)
        def _():
            w_second()

        @pl.when(i == 6)
        def _():
            w_block(0)

        @pl.when(i == chunks + 3)
        def _():
            w_third()

    def z_copy(k, direction, stage):
        sign = 1 - 2 * direction
        if stage == 0:
            part = pl.ds(direction * half, half)
            src, dst = zout.at[k, direction, 0, :, part], zin.at[k, direction, 0, :, part]
        else:
            src, dst = zout.at[k, direction, stage], zin.at[k, direction, stage]
        return remote(src, dst, z_send.at[k, direction, stage], z_recv.at[k, direction, stage], me.at_z(sign))

    def z_stage(k, stage):
        for direction in (0, 1):
            sign = 1 - 2 * direction
            block = mod(me.z + sign * (4 - stage), NZ)
            if stage == 0:
                part = slice(direction * half, (direction + 1) * half)
                zout[k, direction, 0, :, part] = gbuf[k, block, :, part].astype(BF16)
            else:
                z_copy(k, direction, stage - 1).wait_recv()
                if stage == 1:
                    near = slice(direction * half, (direction + 1) * half)
                    rest = slice((1 - direction) * half, (2 - direction) * half)
                    summed = gbuf[k, block, :, near] + zin[k, direction, 0, :, near].astype(F32)
                    zout[k, direction, 1, :, near] = summed.astype(BF16)
                    zout[k, direction, 1, :, rest] = gbuf[k, block, :, rest].astype(BF16)
                else:
                    summed = gbuf[k, block] + zin[k, direction, stage - 1].astype(F32)
                    zout[k, direction, stage] = summed.astype(BF16)
            z_copy(k, direction, stage).start()

    def z_finish(k):
        z_copy(k, 0, 3).wait_recv()
        z_copy(k, 1, 3).wait_recv()
        summed = gbuf[k, me.z] + zin[k, 0, 3].astype(F32) + zin[k, 1, 3].astype(F32)
        out_tok[:, cols(k)] = summed.astype(BF16)

    def y_wait(k):
        seven = rbuf.at[k, pl.ds(0, PLANE - 1)]
        remote(seven, seven, y_send.at[k], y_recv.at[k], me.at_y(1, 0)).wait_recv()
        pltpu.make_async_copy(piece(k)(me.plane), rbuf.at[k, me.plane], y_own.at[k]).wait()

    def map_copy(s):
        z = mod(me.z + s, NZ)
        return remote(maps_own.at[z], maps.at[me.z], map_send.at[s], map_recv.at[s], me.at_z(s))

    def prob_grads():
        seven = pbuf.at[pl.ds(0, PLANE - 1)]
        remote(seven, seven, y_send.at[last], y_recv.at[last], me.at_y(1, 0)).wait_recv()
        pltpu.make_async_copy(dp.at[me.plane], pbuf.at[me.plane], y_own.at[last]).wait()
        row = lax.broadcasted_iota(jnp.int32, (ROWS, rows), 0).astype(F32)
        for d in range(PLANE):
            given = unfold(pbuf[d])
            for z in range(NZ):
                taken = key[d : d + 1, z * rows : (z + 1) * rows] == row
                maps_own[z, d : d + 1, :] = jnp.sum(jnp.where(taken, given, 0.0), axis=0, keepdims=True)
        maps[me.z] = maps_own[me.z]
        for s in range(1, NZ):
            map_copy(s).start()

    def step(i, carry):
        @pl.when(i + 2 < chunks)
        def _():
            y_start(i + 2)

        for stage in (1, 2, 3):

            @pl.when((i >= 2 + stage) & (i < chunks + 2 + stage))
            def _(stage=stage):
                z_stage(i - 2 - stage, stage)

        @pl.when((i >= 2) & (i <= chunks + 1))
        def _():
            k = i - 2
            y_wait(k)
            got = rbuf[k].reshape(PLANE * ROWS, cw)
            gbuf[k] = jnp.dot(spread[...], got, preferred_element_type=F32).reshape(NZ, rows, cw)
            z_stage(k, 0)

        @pl.when((i >= 6) & (i < chunks + 6))
        def _():
            z_finish(i - 6)

        @pl.when(i == 3)
        def _():
            prob_grads()

        w_work(i)
        return carry

    lax.fori_loop(0, chunks + 6, step, 0)
    for s in range(1, NZ):
        z = mod(me.z - s, NZ)
        remote(maps.at[z], maps.at[z], map_send.at[s], map_recv.at[s], me.at_z(s)).wait_recv()
    given = maps[...].reshape(NZ * PLANE, rows)
    wanted = routes[...]
    found = []
    for k in range(wanted.shape[0]):
        same = named[...] == wanted[k : k + 1, :]
        found.append(jnp.sum(jnp.where(same, given, 0.0), axis=0, keepdims=True))
    out_prob[...] = jnp.concatenate(found, axis=0).astype(BF16)

    def drain(k, carry):
        for direction in (0, 1):
            for stage in range(4):
                z_copy(k, direction, stage).wait_send()
        seven = rbuf.at[k, pl.ds(0, PLANE - 1)]
        remote(seven, seven, y_send.at[k], y_recv.at[k], me.at_y(1, 0)).wait_send()
        return carry

    lax.fori_loop(0, chunks, drain, 0)
    seven = pbuf.at[pl.ds(0, PLANE - 1)]
    remote(seven, seven, y_send.at[last], y_recv.at[last], me.at_y(1, 0)).wait_send()
    for s in range(1, NZ):
        map_copy(s).wait_send()
    for n in range(3):
        for hop in range(3):
            w_copy(n, hop).wait_send()
        pltpu.make_async_copy(parts[n][3], finals[n], w_out.at[n]).wait()


def combine(rows_in, wide, grads, dp, key, routes, slots):
    total, _, _, cw = rows_in.shape
    chunks = total // 2
    width = chunks * cw
    rows = dp.shape[2]
    depth, ff = wide.shape[0] // NX, wide.shape[1] // 2
    dma = pltpu.SemaphoreType.DMA
    vmem = pl.BlockSpec(memory_space=pltpu.VMEM)
    smem = pl.BlockSpec(memory_space=pltpu.SMEM)
    anyp = pl.BlockSpec(memory_space=pl.ANY)
    shape = jax.ShapeDtypeStruct
    one, two = (depth, ff), (ff, width // NX)
    return pl.pallas_call(
        functools.partial(combine_kernel, width, chunks),
        out_shape=(
            shape((rows, width), BF16),
            shape(routes.shape, BF16),
            shape(one, F32),
            shape(one, F32),
            shape(two, F32),
        ),
        in_specs=[anyp, anyp, anyp, anyp, vmem, vmem, smem],
        out_specs=(vmem, vmem, anyp, anyp, anyp),
        scratch_shapes=[
            pltpu.VMEM((chunks, PLANE, ROWS, cw), BF16),
            pltpu.VMEM((NZ * rows, PLANE * ROWS), BF16),
            pltpu.VMEM((chunks, NZ, rows, cw), F32),
            pltpu.VMEM((chunks, 2, 4, rows, cw), BF16),
            pltpu.VMEM((chunks, 2, 4, rows, cw), BF16),
            pltpu.VMEM((PLANE, 8, rows), F32),
            pltpu.VMEM((NZ, PLANE, rows), F32),
            pltpu.VMEM((NZ, PLANE, rows), F32),
            pltpu.VMEM(rows_in.shape, BF16),
            pltpu.VMEM(wide.shape, BF16),
            pltpu.VMEM(grads.shape, BF16),
            pltpu.VMEM((chunks, PLANE, ROWS, cw), BF16),
            pltpu.VMEM((NZ * PLANE, rows), jnp.int32),
            pltpu.VMEM(one, F32),
            pltpu.VMEM(one, F32),
            pltpu.VMEM(two, F32),
            pltpu.VMEM((3,) + one, BF16),
            pltpu.VMEM((3,) + one, BF16),
            pltpu.VMEM((3,) + two, BF16),
            pltpu.VMEM((3,) + one, BF16),
            pltpu.VMEM((3,) + one, BF16),
            pltpu.VMEM((3,) + two, BF16),
            dma((NZ,)),
            dma((NZ,)),
            dma((chunks, 2, 4)),
            dma((chunks, 2, 4)),
            dma((chunks + 1,)),
            dma((chunks + 1,)),
            dma((chunks + 1,)),
            dma((3, 3)),
            dma((3, 3)),
            pltpu.VMEM(one, F32),
            pltpu.VMEM(one, F32),
            pltpu.VMEM(two, F32),
            dma((chunks + 2,)),
            dma((3,)),
        ],
        compiler_params=pltpu.CompilerParams(
            collective_id=1, has_side_effects=True, vmem_limit_bytes=67043328
        ),
        name="combine",
    )(rows_in, wide, grads, dp, key, routes, slots)


def hand_over_kernel(*refs):
    half = len(refs) // 2
    for src, dst in zip(refs[:half], refs[half:]):
        dst[...] = src[...]


def hand_over(*arrays, steps=4):
    specs = []
    for array in arrays:
        count = array.shape[0]
        if count >= 8 * steps:
            specs.append(pl.BlockSpec((count // steps, array.shape[1]), lambda i: (i, 0)))
        else:
            specs.append(pl.BlockSpec(array.shape, lambda i: (0, 0)))
    return pl.pallas_call(
        hand_over_kernel,
        grid=(steps,),
        out_shape=tuple(jax.ShapeDtypeStruct(array.shape, array.dtype) for array in arrays),
        in_specs=specs,
        out_specs=tuple(specs),
        name="hand_over",
    )(*arrays)


def shards(tokens, cotangent, routes, probs, slot_expert, gate_w, up_w, down_w):
    rows_in, wide, grads, dp, key = dispatch(
        tokens, cotangent, routes.T, probs.T, slot_expert, gate_w[0], up_w[0], down_w[0]
    )
    grad_tokens, grad_probs, grad_gate, grad_up, grad_down = hand_over(
        *combine(rows_in, wide, grads, dp, key, routes.T, slot_expert)
    )
    return (
        grad_tokens,
        grad_probs.T,
        grad_gate[None],
        grad_up[None],
        grad_down[None],
    )


def solution(mesh):
    placed = (
        P(("dp", "expert"), None),
        P(("dp", "expert"), None),
        P(("dp", "expert"), None),
        P(("dp", "expert"), None),
        P(),
        P("expert", "dp", None),
        P("expert", "dp", None),
        P("expert", None, "dp"),
    )
    return jax.shard_map(
        shards,
        mesh=mesh,
        in_specs=placed,
        out_specs=(
            P(("dp", "expert"), None),
            P(("dp", "expert"), None),
            P("expert", "dp", None),
            P("expert", "dp", None),
            P("expert", None, "dp"),
        ),
        check_vma=False,
    )
```

```python
import functools

import jax
import jax.numpy as jnp
from jax import lax
from jax.experimental import pallas as pl
from jax.experimental.pallas import tpu as pltpu
from jax.sharding import PartitionSpec as P

CAP = 18
NX, NY, NZ, NC = 4, 4, 8, 2
PLANE = NY * NC
ROWS = NZ * CAP
LAG = 8
W_PASS = 9
W_USE = 14
MESH = pl.DeviceIdType.MESH
F32 = jnp.float32
BF16 = jnp.bfloat16


def mod(a, n):
    return lax.rem(a + n, n)


class Place:
    def __init__(self):
        self.x = lax.axis_index("dp")
        e = lax.axis_index("expert")
        self.c = lax.rem(e, NC)
        self.z = lax.rem(lax.div(e, NC), NZ)
        self.y = lax.div(e, NC * NZ)
        self.plane = self.y * NC + self.c

    def dev(self, y, z, c):
        return {"expert": (y * NZ + z) * NC + c}

    def at_z(self, step):
        return self.dev(self.y, mod(self.z + step, NZ), self.c)

    def at_y(self, step, c):
        return self.dev(mod(self.y + step, NY), self.z, c)

    def at_x(self, step):
        return {"dp": mod(self.x + step, NX)}

    def peers(self):
        out = [self.at_z(s) for s in range(1, NZ)]
        out += [self.at_y(s, c) for s in (1, 2, 3) for c in range(NC)]
        out += [self.at_y(0, 1 - self.c), self.at_x(1), self.at_x(-1)]
        return out


def hail(me):
    for peer in me.peers():
        pl.semaphore_signal(pltpu.get_barrier_semaphore(), inc=1, device_id=peer, device_id_type=MESH)


def met(me):
    pl.semaphore_wait(pltpu.get_barrier_semaphore(), len(me.peers()))


def diagonal(count, lanes):
    down = lax.broadcasted_iota(jnp.int32, (count, lanes), 0)
    return down == lax.broadcasted_iota(jnp.int32, (count, lanes), 1)


def fold(column, lanes):
    rest = ROWS - lanes
    first = jnp.sum(jnp.where(diagonal(lanes, lanes), column[:lanes], 0.0), axis=0, keepdims=True)
    second = jnp.sum(jnp.where(diagonal(rest, lanes), column[lanes:], 0.0), axis=0, keepdims=True)
    return jnp.concatenate([first, second, jnp.zeros((6, lanes), F32)], axis=0)


def unfold(tile):
    lanes = tile.shape[1]
    first = jnp.sum(jnp.where(diagonal(lanes, lanes), tile[0:1], 0.0), axis=1, keepdims=True)
    second = jnp.sum(jnp.where(diagonal(ROWS - lanes, lanes), tile[1:2], 0.0), axis=1, keepdims=True)
    return jnp.broadcast_to(jnp.concatenate([first, second], axis=0), (ROWS, lanes))


def remote(src, dst, send, recv, dev):
    return pltpu.make_async_remote_copy(
        src_ref=src, dst_ref=dst, send_sem=send, recv_sem=recv, device_id=dev, device_id_type=MESH
    )


def plane_send(me, piece, landing, send, recv):
    for step in (2, 1, -1):
        for core in range(NC):
            there = mod(me.y + step, NY)
            remote(piece(there * NC + core), landing(me.plane), send, recv, me.at_y(step, core)).start()
    remote(piece(me.y * NC + 1 - me.c), landing(me.plane), send, recv, me.at_y(0, 1 - me.c)).start()


def slot_rows(slot_expert, named):
    for z in range(NZ):
        for y in range(NY):
            for c in range(NC):
                at = z * PLANE + y * NC + c
                named[at : at + 1, :] = jnp.full((1, named.shape[1]), slot_expert[(y * NZ + z) * NC + c], jnp.int32)


def dispatch_kernel(
    width,
    chunks,
    tok,
    cot,
    routes,
    probs,
    slots,
    gate,
    up,
    down,
    out_rows,
    out_wide,
    out_grads,
    out_dp,
    key_out,
    zbuf,
    sbuf,
    landed,
    wide,
    tall,
    acc,
    racc,
    grads,
    dp,
    pin,
    share_of,
    named,
    maps_own,
    maps,
    pick,
    pbuf,
    own_sem,
    map_send,
    map_recv,
    z_send,
    z_recv,
    y_send,
    y_recv,
    y_own,
    w_send,
    w_recv,
    w_own,
    out_sem,
):
    me = Place()
    cw = width // chunks
    half = cw // 2
    ff = gate.shape[1]
    depth = gate.shape[0]
    total = 2 * chunks
    rows = tok.shape[0]

    hail(me)

    def own_copy(k):
        src = (tok, cot)[k // chunks]
        return pltpu.make_async_copy(
            src.at[:, pl.ds((k % chunks) * cw, cw)], zbuf.at[k, me.z], own_sem.at[k]
        )

    for k in range(total):
        own_copy(k).start()

    hit = jnp.zeros((NZ * PLANE, rows), F32)
    weight = jnp.zeros((NZ * PLANE, rows), F32)
    slot_rows(slots, named)
    turned = routes[...]
    shares = probs[...].astype(F32)
    for k in range(turned.shape[0]):
        same = named[...] == turned[k : k + 1, :]
        hit = hit + jnp.where(same, 1.0, 0.0)
        weight = weight + jnp.where(same, shares[k : k + 1, :], 0.0)
    before = lax.broadcasted_iota(jnp.int32, (rows, rows), 0) < lax.broadcasted_iota(
        jnp.int32, (rows, rows), 1
    )
    rank = jnp.dot(
        hit.astype(BF16), jnp.where(before, 1.0, 0.0).astype(BF16), preferred_element_type=F32
    )
    row_of = jnp.where(hit > 0.5, rank + (me.z * CAP).astype(F32), -1.0)
    for z in range(NZ):
        maps_own[z, 0] = row_of[z * PLANE : (z + 1) * PLANE]
        maps_own[z, 1] = weight[z * PLANE : (z + 1) * PLANE]
    maps[me.z] = maps_own[me.z]
    for k in range(total):
        own_copy(k).wait()

    met(me)

    def z_copy(k, direction, stage):
        sign = 1 - 2 * direction
        block = mod(me.z - sign * stage, NZ)
        if stage == 3:
            where = zbuf.at[k, block, :, pl.ds(direction * half, half)]
        else:
            where = zbuf.at[k, block]
        return remote(
            where, where, z_send.at[k, direction, stage], z_recv.at[k, direction, stage], me.at_z(sign)
        )

    def z_wait(k, direction, stage):
        sign = 1 - 2 * direction
        block = mod(me.z - sign * (stage + 1), NZ)
        if stage == 3:
            where = zbuf.at[k, block, :, pl.ds(direction * half, half)]
        else:
            where = zbuf.at[k, block]
        remote(
            where, where, z_send.at[k, direction, stage], z_recv.at[k, direction, stage], me.at_z(sign)
        ).wait_recv()

    def z_stage(k, stage):
        for direction in (0, 1):
            if stage > 0:
                z_wait(k, direction, stage - 1)
            if stage < 4:
                z_copy(k, direction, stage).start()

    weights = (gate, up, down)

    def w_slot(n, owner):
        if n < 2:
            return wide.at[pl.ds(pl.multiple_of(owner * depth, 128), depth), pl.ds(n * ff, ff)]
        part = down.shape[1]
        return tall.at[:, pl.ds(pl.multiple_of(owner * part, 128), part)]

    def w_copy(n, direction, hop):
        sign = 1 - 2 * direction
        owner = me.x if hop == 0 else mod(me.x - sign, NX)
        src = weights[n] if hop == 0 else w_slot(n, owner)
        return remote(
            src, w_slot(n, owner), w_send.at[n, direction, hop], w_recv.at[n, direction, hop], me.at_x(sign)
        )

    def w_wait(n, direction, hop):
        sign = 1 - 2 * direction
        slot = w_slot(n, mod(me.x - sign * (hop + 1), NX))
        remote(
            slot, slot, w_send.at[n, direction, hop], w_recv.at[n, direction, hop], me.at_x(sign)
        ).wait_recv()

    for s in range(1, NZ):
        z = mod(me.z + s, NZ)
        remote(maps_own.at[z], maps.at[me.z], map_send.at[s], map_recv.at[s], me.at_z(s)).start()
    z_stage(0, 0)
    for n in range(3):
        for direction in (0, 1):
            w_copy(n, direction, 0).start()
        pltpu.make_async_copy(weights[n], w_slot(n, me.x), w_own.at[n]).start()

    def choose(d):
        row = lax.broadcasted_iota(jnp.int32, (ROWS, rows), 0).astype(F32)
        share = jnp.zeros((ROWS, rows), F32)
        for z in range(NZ):
            taken = maps[z, 0, d : d + 1, :] == row
            pick[d * ROWS : (d + 1) * ROWS, z * rows : (z + 1) * rows] = jnp.where(taken, 1.0, 0.0).astype(BF16)
            share = share + jnp.where(taken, maps[z, 1, d : d + 1, :], 0.0)
            key_out[d : d + 1, z * rows : (z + 1) * rows] = maps[z, 0, d : d + 1, :]
        pbuf[d] = fold(jnp.sum(share, axis=1, keepdims=True), rows)

    last = total

    def piece(k):
        return lambda d: sbuf.at[k, d]

    def landing(k):
        return lambda slot: landed.at[k, slot]

    def own_rows(k):
        return pltpu.make_async_copy(sbuf.at[k, me.plane], landed.at[k, me.plane], y_own.at[k])

    def send_chunk(k):
        plane_send(me, piece(k), landing(k), y_send.at[k], y_recv.at[k])
        own_rows(k).start()

    def seven_of(k):
        sent, here = sbuf.at[k, pl.ds(0, PLANE - 1)], landed.at[k, pl.ds(0, PLANE - 1)]
        return remote(sent, here, y_send.at[k], y_recv.at[k], me.at_y(1, 0))

    def rows_out(k):
        return pltpu.make_async_copy(landed.at[k], out_rows.at[k], out_sem.at[k])

    def consume_x(k):
        seven_of(k).wait_recv()
        own_rows(k).wait()
        take = pl.ds(pl.multiple_of(k * cw, cw), cw)
        acc[...] += jnp.dot(landed[k].reshape(PLANE * ROWS, cw), wide[take, :], preferred_element_type=F32)
        rows_out(k).start()

    def consume_dy(k):
        seven_of(k).wait_recv()
        own_rows(k).wait()
        take = pl.ds(pl.multiple_of((k - chunks) * cw, cw), cw)
        racc[...] += lax.dot_general(
            landed[k].reshape(PLANE * ROWS, cw),
            tall[:, take],
            (((1,), (1,)), ((), ())),
            preferred_element_type=F32,
        )
        for d in range(PLANE):
            for j in range(cw // rows):
                part = slice(j * rows, (j + 1) * rows)
                scaled = landed[k, d, :, part].astype(F32) * share_of[d]
                landed[k, d, :, part] = scaled.astype(BF16)
        rows_out(k).start()

    def p_land(slot):
        return pin.at[slot]

    def wide_out(n):
        if n == 0:
            return pltpu.make_async_copy(wide, out_wide, out_sem.at[total])
        return pltpu.make_async_copy(grads, out_grads, out_sem.at[total + 1])

    def p_seven():
        sent, here = pbuf.at[pl.ds(0, PLANE - 1)], pin.at[pl.ds(0, PLANE - 1)]
        return remote(sent, here, y_send.at[last], y_recv.at[last], me.at_y(1, 0))

    def step(i, carry):
        @pl.when((i >= 4) & (i < total + 4))
        def _():
            k = i - 4
            z_stage(k, 4)
            block = zbuf[k].reshape(NZ * rows, cw)
            out = jnp.dot(pick[...], block, preferred_element_type=F32).astype(BF16)
            sbuf[k] = out.reshape(PLANE, ROWS, cw)
            send_chunk(k)

        for stage in (3, 2, 1):

            @pl.when((i >= stage) & (i < total + stage))
            def _(stage=stage):
                z_stage(i - stage, stage)

        @pl.when((i >= 1) & (i < total))
        def _():
            z_stage(i, 0)

        @pl.when(i == 0)
        def _():
            for s in range(1, NZ):
                z = mod(me.z - s, NZ)
                remote(maps.at[z], maps.at[z], map_send.at[s], map_recv.at[s], me.at_z(s)).wait_recv()

        for turn in range(4):

            @pl.when(i == turn)
            def _(turn=turn):
                choose(2 * turn)
                choose(2 * turn + 1)

        @pl.when(i == 6)
        def _():
            acc[...] = jnp.zeros_like(acc)
            racc[...] = jnp.zeros_like(racc)

        @pl.when(i == 4)
        def _():
            plane_send(me, lambda d: pbuf.at[d], p_land, y_send.at[last], y_recv.at[last])
            pltpu.make_async_copy(pbuf.at[me.plane], pin.at[me.plane], y_own.at[last]).start()

        @pl.when(i == W_PASS)
        def _():
            for n in range(3):
                for direction in (0, 1):
                    w_wait(n, direction, 0)
                w_copy(n, 0 if n < 2 else 1, 1).start()

        @pl.when(i == W_USE)
        def _():
            for n in range(3):
                w_wait(n, 0 if n < 2 else 1, 1)
                pltpu.make_async_copy(weights[n], w_slot(n, me.x), w_own.at[n]).wait()
            wide_out(0).start()
            p_seven().wait_recv()
            pltpu.make_async_copy(pbuf.at[me.plane], pin.at[me.plane], y_own.at[last]).wait()
            for d in range(PLANE):
                share_of[d] = unfold(pin[d])

        @pl.when((i >= W_USE) & (i < chunks + W_USE))
        def _():
            consume_x(i - W_USE)

        @pl.when((i >= chunks + LAG) & (i < total + LAG))
        def _():
            consume_dy(i - LAG)

        return carry

    lax.fori_loop(0, total + LAG, step, 0)

    def point(d, carry):
        these = pl.ds(pl.multiple_of(d * ROWS, 16), ROWS)
        g, u, r = acc[these, :ff], acc[these, ff:], racc[these, :]
        p = share_of[d]
        p = jnp.concatenate([p] * (ff // rows), axis=1)
        sg = jax.nn.sigmoid(g)
        act = g * sg
        hidden = (act * u).astype(BF16)
        given = jnp.sum(hidden.astype(F32) * r, axis=1, keepdims=True)
        dp[d] = fold(given.astype(BF16).astype(F32), rows)
        dh = p * r
        grads[these, :ff] = (dh * u * sg * (1.0 + g * (1.0 - sg))).astype(BF16)
        grads[these, ff : 2 * ff] = (dh * act).astype(BF16)
        grads[these, 2 * ff :] = hidden
        pltpu.make_async_copy(grads.at[these], out_grads.at[these], out_sem.at[total + 1]).start()
        return carry

    lax.fori_loop(0, PLANE, point, 0)
    dp_out = pltpu.make_async_copy(dp, out_dp, out_sem.at[total + 2])
    dp_out.start()

    for n in range(3):
        for direction in (0, 1):
            w_copy(n, direction, 0).wait_send()
        w_copy(n, 0 if n < 2 else 1, 1).wait_send()
    for s in range(1, NZ):
        z = mod(me.z + s, NZ)
        remote(maps_own.at[z], maps.at[me.z], map_send.at[s], map_recv.at[s], me.at_z(s)).wait_send()

    def drain(k, carry):
        for direction in (0, 1):
            for stage in range(4):
                z_copy(k, direction, stage).wait_send()
        seven_of(k).wait_send()
        rows_out(k).wait()
        return carry

    lax.fori_loop(0, total, drain, 0)
    p_seven().wait_send()
    wide_out(0).wait()
    wide_out(1).wait()
    dp_out.wait()


def dispatch(tokens, cotangent, routes, probs, slots, gate, up, down, chunks=8):
    rows, width = tokens.shape
    depth, ff = gate.shape
    cw, total = width // chunks, 2 * chunks
    dma = pltpu.SemaphoreType.DMA
    vmem = pl.BlockSpec(memory_space=pltpu.VMEM)
    anyp = pl.BlockSpec(memory_space=pl.ANY)
    shape = jax.ShapeDtypeStruct
    return pl.pallas_call(
        functools.partial(dispatch_kernel, width, chunks),
        out_shape=(
            shape((total, PLANE, ROWS, cw), BF16),
            shape((NX * depth, 2 * ff), BF16),
            shape((PLANE * ROWS, 3 * ff), BF16),
            shape((PLANE, 8, rows), F32),
            shape((PLANE, NZ * rows), F32),
        ),
        in_specs=[anyp, anyp, vmem, vmem, pl.BlockSpec(memory_space=pltpu.SMEM), vmem, vmem, vmem],
        out_specs=(anyp, anyp, anyp, anyp, vmem),
        scratch_shapes=[
            pltpu.VMEM((total, NZ, rows, cw), BF16),
            pltpu.VMEM((total, PLANE, ROWS, cw), BF16),
            pltpu.VMEM((total, PLANE, ROWS, cw), BF16),
            pltpu.VMEM((NX * depth, 2 * ff), BF16),
            pltpu.VMEM((ff, width), BF16),
            pltpu.VMEM((PLANE * ROWS, 2 * ff), F32),
            pltpu.VMEM((PLANE * ROWS, ff), F32),
            pltpu.VMEM((PLANE * ROWS, 3 * ff), BF16),
            pltpu.VMEM((PLANE, 8, rows), F32),
            pltpu.VMEM((PLANE, 8, rows), F32),
            pltpu.VMEM((PLANE, ROWS, rows), F32),
            pltpu.VMEM((NZ * PLANE, rows), jnp.int32),
            pltpu.VMEM((NZ, 2, PLANE, rows), F32),
            pltpu.VMEM((NZ, 2, PLANE, rows), F32),
            pltpu.VMEM((PLANE * ROWS, NZ * rows), BF16),
            pltpu.VMEM((PLANE, 8, rows), F32),
            dma((total,)),
            dma((NZ,)),
            dma((NZ,)),
            dma((total, 2, 4)),
            dma((total, 2, 4)),
            dma((total + 1,)),
            dma((total + 1,)),
            dma((total + 1,)),
            dma((3, 2, 2)),
            dma((3, 2, 2)),
            dma((3,)),
            dma((total + 3,)),
        ],
        compiler_params=pltpu.CompilerParams(
            collective_id=0, has_side_effects=True, vmem_limit_bytes=60 * 1024 * 1024
        ),
        name="dispatch",
    )(tokens, cotangent, routes, probs, slots, gate, up, down)


def combine_kernel(
    width,
    chunks,
    rows_in,
    wide_in,
    grads_in,
    dp,
    key,
    routes,
    slots,
    out_tok,
    out_prob,
    out_gate,
    out_up,
    out_down,
    rbuf,
    spread,
    gbuf,
    zout,
    zin,
    pbuf,
    maps_own,
    maps,
    kept,
    wide,
    grads,
    dx,
    named,
    wmid0,
    wmid1,
    wmid2,
    wout0,
    wout1,
    wout2,
    win0,
    win1,
    win2,
    map_send,
    map_recv,
    z_send,
    z_recv,
    y_send,
    y_recv,
    y_own,
    w_send,
    w_recv,
    own0,
    own1,
    own2,
    load_sem,
    w_out,
):
    me = Place()
    cw = width // chunks
    half = cw // 2
    ff = out_gate.shape[1]
    per = width // NX // cw
    rows = out_tok.shape[0]
    last = chunks
    parts = ((wmid0, wout0, win0, own0), (wmid1, wout1, win1, own1), (wmid2, wout2, win2, own2))
    finals = (out_gate, out_up, out_down)
    way = (1, -1, 1)

    def load(n):
        if n < chunks:
            take = pl.ds(n * cw, cw)
            return pltpu.make_async_copy(wide_in.at[take], wide.at[take], load_sem.at[n])
        if n == chunks:
            return pltpu.make_async_copy(grads_in, grads, load_sem.at[n])
        return pltpu.make_async_copy(rows_in, kept, load_sem.at[n])

    hail(me)
    load(chunks).start()
    for n in range(chunks):
        load(n).start()
    load(chunks + 1).start()

    met(me)

    def cols(k):
        return pl.ds(pl.multiple_of(k * cw, cw), cw)

    def piece(k):
        return lambda d: dx.at[k, d]

    def landing(k):
        return lambda slot: rbuf.at[k, slot]

    def y_start(k):
        out = lax.dot_general(
            grads[:, : 2 * ff], wide[cols(k), :], (((1,), (1,)), ((), ())), preferred_element_type=F32
        )
        dx[k] = out.astype(BF16).reshape(PLANE, ROWS, cw)
        plane_send(me, piece(k), landing(k), y_send.at[k], y_recv.at[k])
        pltpu.make_async_copy(piece(k)(me.plane), rbuf.at[k, me.plane], y_own.at[k]).start()

    def p_land(slot):
        return pbuf.at[slot]

    plane_send(me, lambda d: dp.at[d], p_land, y_send.at[last], y_recv.at[last])
    pltpu.make_async_copy(dp.at[me.plane], pbuf.at[me.plane], y_own.at[last]).start()
    load(chunks).wait()
    load(0).wait()
    y_start(0)
    load(1).wait()
    y_start(1)
    for n in range(2, chunks):
        load(n).wait()
    slot_rows(slots, named)

    lane = lax.broadcasted_iota(jnp.int32, (NZ * rows, 128), 1).astype(F32)
    turned = key[...].T
    for j in range(PLANE * ROWS // 128):
        tile = jnp.zeros((NZ * rows, 128), F32)
        for d in range(128 * j // ROWS, (128 * j + 127) // ROWS + 1):
            mine = turned[:, d : d + 1]
            where = jnp.where(mine >= 0.0, mine + float(d * ROWS - 128 * j), -1.0)
            tile = tile + jnp.where(where == lane, 1.0, 0.0)
        spread[:, j * 128 : (j + 1) * 128] = tile.astype(BF16)

    def w_copy(n, hop):
        sign = way[n] if hop < 2 else -way[n]
        return remote(
            parts[n][1].at[hop], parts[n][2].at[hop], w_send.at[n, hop], w_recv.at[n, hop], me.at_x(sign)
        )

    def put(n, off, j, value):
        where = (slice(j * cw, (j + 1) * cw), slice(None))
        if n == 2:
            where = where[::-1]
        if off == 0:
            parts[n][3][where] = value
        elif off == way[n]:
            parts[n][0][where] = value
        else:
            parts[n][1][(0 if off == 2 else 2,) + where] = value.astype(BF16)

    def w_block(off):
        owner = mod(me.x + off, NX)
        down_to = (((0,), (0,)), ((), ()))
        for j in range(per):
            x = kept[owner * per + j].reshape(PLANE * ROWS, cw)
            w = kept[chunks + owner * per + j].reshape(PLANE * ROWS, cw)
            both = lax.dot_general(x, grads[:, : 2 * ff], down_to, preferred_element_type=F32)
            put(0, off, j, both[:, :ff])
            put(1, off, j, both[:, ff:])
            put(2, off, j, lax.dot_general(grads[:, 2 * ff :], w, down_to, preferred_element_type=F32))

    def w_second():
        for n in range(3):
            w_copy(n, 0).wait_recv()
            summed = parts[n][0][...] + parts[n][2][0].astype(F32)
            parts[n][1][1] = summed.astype(BF16)
        for n in range(3):
            w_copy(n, 1).start()

    def w_third():
        for n in range(3):
            w_copy(n, 1).wait_recv()
            w_copy(n, 2).wait_recv()
            parts[n][3][...] += parts[n][2][1].astype(F32) + parts[n][2][2].astype(F32)
            pltpu.make_async_copy(parts[n][3], finals[n], w_out.at[n]).start()

    def w_work(i):
        @pl.when(i == 0)
        def _():
            load(chunks + 1).wait()
            w_block(2)
            for n in range(3):
                w_copy(n, 0).start()

        @pl.when(i == 1)
        def _():
            w_block(1)
            w_copy(1, 2).start()

        @pl.when(i == 2)
        def _():
            w_block(-1)
            w_copy(0, 2).start()
            w_copy(2, 2).start()

        @pl.when(i == 4)
        def _():
            w_second()

        @pl.when(i == 6)
        def _():
            w_block(0)

        @pl.when(i == chunks + 3)
        def _():
            w_third()

    def z_copy(k, direction, stage):
        sign = 1 - 2 * direction
        if stage == 0:
            part = pl.ds(direction * half, half)
            src, dst = zout.at[k, direction, 0, :, part], zin.at[k, direction, 0, :, part]
        else:
            src, dst = zout.at[k, direction, stage], zin.at[k, direction, stage]
        return remote(src, dst, z_send.at[k, direction, stage], z_recv.at[k, direction, stage], me.at_z(sign))

    def z_stage(k, stage):
        for direction in (0, 1):
            sign = 1 - 2 * direction
            block = mod(me.z + sign * (4 - stage), NZ)
            if stage == 0:
                part = slice(direction * half, (direction + 1) * half)
                zout[k, direction, 0, :, part] = gbuf[k, block, :, part].astype(BF16)
            else:
                z_copy(k, direction, stage - 1).wait_recv()
                if stage == 1:
                    near = slice(direction * half, (direction + 1) * half)
                    rest = slice((1 - direction) * half, (2 - direction) * half)
                    summed = gbuf[k, block, :, near] + zin[k, direction, 0, :, near].astype(F32)
                    zout[k, direction, 1, :, near] = summed.astype(BF16)
                    zout[k, direction, 1, :, rest] = gbuf[k, block, :, rest].astype(BF16)
                else:
                    summed = gbuf[k, block] + zin[k, direction, stage - 1].astype(F32)
                    zout[k, direction, stage] = summed.astype(BF16)
            z_copy(k, direction, stage).start()

    def z_finish(k):
        z_copy(k, 0, 3).wait_recv()
        z_copy(k, 1, 3).wait_recv()
        summed = gbuf[k, me.z] + zin[k, 0, 3].astype(F32) + zin[k, 1, 3].astype(F32)
        out_tok[:, cols(k)] = summed.astype(BF16)

    def y_wait(k):
        seven = rbuf.at[k, pl.ds(0, PLANE - 1)]
        remote(seven, seven, y_send.at[k], y_recv.at[k], me.at_y(1, 0)).wait_recv()
        pltpu.make_async_copy(piece(k)(me.plane), rbuf.at[k, me.plane], y_own.at[k]).wait()

    def map_copy(s):
        z = mod(me.z + s, NZ)
        return remote(maps_own.at[z], maps.at[me.z], map_send.at[s], map_recv.at[s], me.at_z(s))

    def prob_grads():
        seven = pbuf.at[pl.ds(0, PLANE - 1)]
        remote(seven, seven, y_send.at[last], y_recv.at[last], me.at_y(1, 0)).wait_recv()
        pltpu.make_async_copy(dp.at[me.plane], pbuf.at[me.plane], y_own.at[last]).wait()
        row = lax.broadcasted_iota(jnp.int32, (ROWS, rows), 0).astype(F32)
        for d in range(PLANE):
            given = unfold(pbuf[d])
            for z in range(NZ):
                taken = key[d : d + 1, z * rows : (z + 1) * rows] == row
                maps_own[z, d : d + 1, :] = jnp.sum(jnp.where(taken, given, 0.0), axis=0, keepdims=True)
        maps[me.z] = maps_own[me.z]
        for s in range(1, NZ):
            map_copy(s).start()

    def step(i, carry):
        @pl.when(i + 2 < chunks)
        def _():
            y_start(i + 2)

        for stage in (1, 2, 3):

            @pl.when((i >= 2 + stage) & (i < chunks + 2 + stage))
            def _(stage=stage):
                z_stage(i - 2 - stage, stage)

        @pl.when((i >= 2) & (i <= chunks + 1))
        def _():
            k = i - 2
            y_wait(k)
            got = rbuf[k].reshape(PLANE * ROWS, cw)
            gbuf[k] = jnp.dot(spread[...], got, preferred_element_type=F32).reshape(NZ, rows, cw)
            z_stage(k, 0)

        @pl.when((i >= 6) & (i < chunks + 6))
        def _():
            z_finish(i - 6)

        @pl.when(i == 3)
        def _():
            prob_grads()

        w_work(i)
        return carry

    lax.fori_loop(0, chunks + 6, step, 0)
    for s in range(1, NZ):
        z = mod(me.z - s, NZ)
        remote(maps.at[z], maps.at[z], map_send.at[s], map_recv.at[s], me.at_z(s)).wait_recv()
    given = maps[...].reshape(NZ * PLANE, rows)
    wanted = routes[...]
    found = []
    for k in range(wanted.shape[0]):
        same = named[...] == wanted[k : k + 1, :]
        found.append(jnp.sum(jnp.where(same, given, 0.0), axis=0, keepdims=True))
    out_prob[...] = jnp.concatenate(found, axis=0).astype(BF16)

    def drain(k, carry):
        for direction in (0, 1):
            for stage in range(4):
                z_copy(k, direction, stage).wait_send()
        seven = rbuf.at[k, pl.ds(0, PLANE - 1)]
        remote(seven, seven, y_send.at[k], y_recv.at[k], me.at_y(1, 0)).wait_send()
        return carry

    lax.fori_loop(0, chunks, drain, 0)
    seven = pbuf.at[pl.ds(0, PLANE - 1)]
    remote(seven, seven, y_send.at[last], y_recv.at[last], me.at_y(1, 0)).wait_send()
    for s in range(1, NZ):
        map_copy(s).wait_send()
    for n in range(3):
        for hop in range(3):
            w_copy(n, hop).wait_send()
        pltpu.make_async_copy(parts[n][3], finals[n], w_out.at[n]).wait()


def combine(rows_in, wide, grads, dp, key, routes, slots):
    total, _, _, cw = rows_in.shape
    chunks = total // 2
    width = chunks * cw
    rows = dp.shape[2]
    depth, ff = wide.shape[0] // NX, wide.shape[1] // 2
    dma = pltpu.SemaphoreType.DMA
    vmem = pl.BlockSpec(memory_space=pltpu.VMEM)
    smem = pl.BlockSpec(memory_space=pltpu.SMEM)
    anyp = pl.BlockSpec(memory_space=pl.ANY)
    shape = jax.ShapeDtypeStruct
    one, two = (depth, ff), (ff, width // NX)
    return pl.pallas_call(
        functools.partial(combine_kernel, width, chunks),
        out_shape=(
            shape((rows, width), BF16),
            shape(routes.shape, BF16),
            shape(one, F32),
            shape(one, F32),
            shape(two, F32),
        ),
        in_specs=[anyp, anyp, anyp, anyp, vmem, vmem, smem],
        out_specs=(vmem, vmem, anyp, anyp, anyp),
        scratch_shapes=[
            pltpu.VMEM((chunks, PLANE, ROWS, cw), BF16),
            pltpu.VMEM((NZ * rows, PLANE * ROWS), BF16),
            pltpu.VMEM((chunks, NZ, rows, cw), F32),
            pltpu.VMEM((chunks, 2, 4, rows, cw), BF16),
            pltpu.VMEM((chunks, 2, 4, rows, cw), BF16),
            pltpu.VMEM((PLANE, 8, rows), F32),
            pltpu.VMEM((NZ, PLANE, rows), F32),
            pltpu.VMEM((NZ, PLANE, rows), F32),
            pltpu.VMEM(rows_in.shape, BF16),
            pltpu.VMEM(wide.shape, BF16),
            pltpu.VMEM(grads.shape, BF16),
            pltpu.VMEM((chunks, PLANE, ROWS, cw), BF16),
            pltpu.VMEM((NZ * PLANE, rows), jnp.int32),
            pltpu.VMEM(one, F32),
            pltpu.VMEM(one, F32),
            pltpu.VMEM(two, F32),
            pltpu.VMEM((3,) + one, BF16),
            pltpu.VMEM((3,) + one, BF16),
            pltpu.VMEM((3,) + two, BF16),
            pltpu.VMEM((3,) + one, BF16),
            pltpu.VMEM((3,) + one, BF16),
            pltpu.VMEM((3,) + two, BF16),
            dma((NZ,)),
            dma((NZ,)),
            dma((chunks, 2, 4)),
            dma((chunks, 2, 4)),
            dma((chunks + 1,)),
            dma((chunks + 1,)),
            dma((chunks + 1,)),
            dma((3, 3)),
            dma((3, 3)),
            pltpu.VMEM(one, F32),
            pltpu.VMEM(one, F32),
            pltpu.VMEM(two, F32),
            dma((chunks + 2,)),
            dma((3,)),
        ],
        compiler_params=pltpu.CompilerParams(
            collective_id=1, has_side_effects=True, vmem_limit_bytes=67043328
        ),
        name="combine",
    )(rows_in, wide, grads, dp, key, routes, slots)


def hand_over_kernel(*refs):
    half = len(refs) // 2
    for src, dst in zip(refs[:half], refs[half:]):
        dst[...] = src[...]


def hand_over(*arrays, steps=2):
    specs = []
    for array in arrays:
        count = array.shape[0]
        if count >= 8 * steps:
            specs.append(pl.BlockSpec((count // steps, array.shape[1]), lambda i: (i, 0)))
        else:
            specs.append(pl.BlockSpec(array.shape, lambda i: (0, 0)))
    return pl.pallas_call(
        hand_over_kernel,
        grid=(steps,),
        out_shape=tuple(jax.ShapeDtypeStruct(array.shape, array.dtype) for array in arrays),
        in_specs=specs,
        out_specs=tuple(specs),
        name="hand_over",
    )(*arrays)


def shards(tokens, cotangent, routes, probs, slot_expert, gate_w, up_w, down_w):
    rows_in, wide, grads, dp, key = dispatch(
        tokens, cotangent, routes.T, probs.T, slot_expert, gate_w[0], up_w[0], down_w[0]
    )
    grad_tokens, grad_probs, grad_gate, grad_up, grad_down = hand_over(
        *combine(rows_in, wide, grads, dp, key, routes.T, slot_expert)
    )
    return (
        grad_tokens,
        grad_probs.T,
        grad_gate[None],
        grad_up[None],
        grad_down[None],
    )


def solution(mesh):
    placed = (
        P(("dp", "expert"), None),
        P(("dp", "expert"), None),
        P(("dp", "expert"), None),
        P(("dp", "expert"), None),
        P(),
        P("expert", "dp", None),
        P("expert", "dp", None),
        P("expert", None, "dp"),
    )
    return jax.shard_map(
        shards,
        mesh=mesh,
        in_specs=placed,
        out_specs=(
            P(("dp", "expert"), None),
            P(("dp", "expert"), None),
            P("expert", "dp", None),
            P("expert", "dp", None),
            P("expert", None, "dp"),
        ),
        check_vma=False,
    )
```
